128 devices in a mesh: dp: 8 (over y, core), feat: 16 (over z, x).
Axes of the slice: x: 4, y: 4, z: 4, core: 2. Of those that a mesh axis runs over, the one named last changes fastest.
Arguments:
- features: bfloat16 [32768, 8192], P('dp', 'feat'), may hold values from -6 to 6
- fixed_coef: float32 [8192], P('feat'), may hold values from -0.0625 to 0.0625
- member_score: float32 [32768], P('dp'), may hold values from -6 to 6
- clicks: int32 [32768], P('dp'), may hold values 0 or 1
- member_features: bfloat16 [32768, 256], P(('dp', 'feat')), may hold values from -6 to 6
- member_coef: float32 [1024, 256], P(('dp', 'feat')), may hold values from -0.375 to 0.375
- block_slot: int32 [32768], P(('dp', 'feat')), may hold values from 0 to 65535, as said below
Outputs:
- fixed_grad: float32 [8192], P('feat')
- member_coef_new: float32 [1024, 256], P(('dp', 'feat'))
- total_score: float32 [32768], P(('dp', 'feat'))
The draws below stay inside these ranges and needn't reach their ends.
Inputs may be any that keep to these rules, and one draw needn't show every extreme that they name: All block_slot values differ. block_slot // 512 is the device (index along dp+feat) that owns the impression's member, and block_slot // 64 is the member. Every owner receives exactly 256 impressions. One device sends at most 6 of its impressions to one owner, and every device sends exactly 6 to some owner.
All inputs are finite; a program needn't handle non-finite values. Where the reference program divides by a largest or mean magnitude, that divisor is 1e-20 or more. No bound on the sum of `clicks` on one device may be relied on, other than what follows from the above.
Results may differ from the reference program's by a relative error of at most 0.0093.
Values may be sent and summed in bfloat16 or wider, within the bound.
A program may use at most 64 MiB of HBM per device.

```python
import math
import jax
import jax.numpy as jnp
from jax import lax

F = 8192
KRE = 256
BLK = 64
NEWTON = 3
IMP_DEV = 256
IMPS = 32768
MEMBERS = 1024
SLOTS = 512
CAP = 6


def draw_block_slot(key, part):
    n_devices = IMPS // IMP_DEV
    key_order, key_slots = jax.random.split(jax.random.fold_in(key, 7))
    shuffled = jax.random.permutation(key_order, n_devices).astype(jnp.int32)
    position = jnp.zeros((n_devices,), jnp.int32).at[shuffled].set(jnp.arange(n_devices, dtype=jnp.int32))
    value = jnp.arange(n_devices, dtype=jnp.int32)
    priority = jnp.where(value == 1, 0, jnp.where(value == n_devices - 1, 1, jnp.where(value == n_devices // 2, 2, 3 + position)))
    offsets = jnp.argsort(priority, stable=True).astype(jnp.int32)
    row_index = jnp.arange(IMP_DEV)
    others = max(n_devices - 1, 1)
    later_rows = jnp.maximum(row_index - CAP, 0)
    offset_of = jnp.where(row_index < CAP, offsets[0], offsets[jnp.minimum(1 + later_rows % others, n_devices - 1)])
    row_rank = jnp.where(row_index < CAP, row_index, later_rows // others)
    counts = jnp.zeros((n_devices,), jnp.int32).at[offset_of].add(1)
    sender = jnp.arange(n_devices)[:, None]
    target = jnp.arange(n_devices)[None, :]
    count_table = counts[(target - sender) % n_devices]
    base_rank = jnp.cumsum(count_table, axis=0) - count_table
    owner_dev = (sender + offset_of[None, :]) % n_devices
    arrival = jnp.take_along_axis(base_rank, owner_dev, axis=1) + row_rank[None, :]
    key_list = jax.random.split(key_slots, n_devices)
    shuffles = jax.vmap(lambda single: jax.random.permutation(single, SLOTS))(key_list)
    local_slot = shuffles[owner_dev, arrival]
    return (owner_dev * SLOTS + local_slot).reshape(-1).astype(jnp.int32)


def place_ends(entries, key, smallest, high):
    spot = [jax.random.randint(jax.random.fold_in(key, axis), (), 0, length) for axis, length in enumerate(entries.shape)]
    longest = entries.shape.index(max(entries.shape))
    neighbour = spot[:longest] + [(spot[longest] + 1) % entries.shape[longest]] + spot[longest + 1:]
    return entries.at[tuple(spot)].set(smallest).at[tuple(neighbour)].set(high)


def levels(stream_key, shape, cuts, least, top_value):
    level = 1.0
    for dim, blocks in cuts:
        steps = jax.random.uniform(jax.random.fold_in(jax.random.fold_in(stream_key, 6), dim), (blocks,), jnp.float32, least / len(cuts), top_value / len(cuts))
        level = level * jnp.repeat(jnp.exp(steps), shape[dim] // blocks).reshape((-1,) + (1,) * (len(shape) - 1 - dim))
    return level


def bell_draw(stream_key, extent, deviation, limit, cuts=(), kind=jnp.bfloat16):
    drawn = jax.random.normal(stream_key, extent, jnp.float32) * deviation
    if len(cuts) > 0:
        drawn = levels(stream_key, extent, cuts, -0.22, 0.18) * drawn
    return jnp.clip(drawn, min=-limit, max=limit).astype(kind)


def setup_inputs(seed: int = 0) -> dict:
    keys = jax.random.split(jax.random.key(seed), 8)
    return {
        "features": bell_draw(keys[0], (IMPS, F), 1.0, 6.0, ((0, 8), (1, 16))),
        "fixed_coef": bell_draw(keys[1], (F,), F ** -0.5, 0.0625, ((0, 16),), jnp.float32),
        "member_score": bell_draw(keys[2], (IMPS,), 1.0, 6.0, ((0, 8),), jnp.float32),
        "clicks": place_ends((jax.random.randint(keys[3], (IMPS,), 0, 4) < 1).astype(jnp.int32), jax.random.fold_in(keys[3], 1), 0, 1),
        "member_features": bell_draw(keys[4], (IMPS, KRE), 1.0, 6.0, ((0, 128),)),
        "member_coef": bell_draw(keys[5], (MEMBERS, KRE), KRE ** -0.5, 0.375, ((0, 128),), jnp.float32),
        "block_slot": draw_block_slot(jax.random.fold_in(keys[7], 71), 0),
    }


ridge_weight = 1.0
high = lax.Precision.HIGHEST
inverse_sweeps = 20

def apply_inverse(system, vector):
    identity = jnp.eye(system.shape[1], dtype=system.dtype)
    bound = lax.optimization_barrier(jnp.max(lax.optimization_barrier(jnp.sum(jnp.abs(system), axis=2)), axis=1))
    start = (2.0 / (1.0 + bound))[:, None, None] * identity[None, :, :]

    def sweep(index, approx):
        product = jnp.einsum('mbc,mcd->mbd', system, approx, precision=high)
        return 2.0 * approx - jnp.einsum('mbc,mcd->mbd', approx, product, precision=high)
    approx = lax.fori_loop(0, inverse_sweeps, sweep, start)
    return jnp.einsum('mbc,mc->mb', approx, vector, precision=high)

def newton_blocks(padded_rows, offset, label_pad, live_pad, coeffs):
    gram_matrix = jnp.einsum('mbk,mck->mbc', padded_rows, padded_rows, precision=high)
    identity = jnp.eye(padded_rows.shape[1], dtype=padded_rows.dtype)
    for iteration in range(NEWTON):
        linear = offset + jnp.einsum('mbk,mk->mb', padded_rows, coeffs, precision=high)
        probability = jax.nn.sigmoid(linear)
        gradient = jnp.einsum('mbk,mb->mk', padded_rows, live_pad * (probability - label_pad), precision=high) + ridge_weight * coeffs
        weight_root = jnp.sqrt(live_pad * probability * (1.0 - probability))
        system = ridge_weight * identity + weight_root[:, :, None] * gram_matrix * weight_root[:, None, :]
        projected = weight_root * jnp.einsum('mbk,mk->mb', padded_rows, gradient, precision=high)
        solved = apply_inverse(system, projected)
        back_term = jnp.einsum('mbk,mb->mk', padded_rows, weight_root * solved, precision=high)
        coeffs = coeffs - (gradient - back_term) / ridge_weight
    return coeffs

def reference(features, fixed_coef, member_score, clicks, member_features, member_coef, block_slot):
    coef_half = fixed_coef.astype(jnp.bfloat16)
    fixed_score = jnp.dot(features, coef_half, preferred_element_type=jnp.float32)
    click_value = clicks.astype(jnp.float32)
    residual = (jax.nn.sigmoid(fixed_score + member_score) - click_value).astype(jnp.bfloat16)
    fixed_grad = jnp.dot(residual, features, preferred_element_type=jnp.float32) / math.sqrt(IMPS)
    slot_total = MEMBERS * BLK
    padded_rows = jnp.zeros((slot_total, KRE), jnp.float32).at[block_slot].set(member_features.astype(jnp.float32)).reshape(MEMBERS, BLK, KRE)
    offset = jnp.zeros((slot_total,), jnp.float32).at[block_slot].set(fixed_score).reshape(MEMBERS, BLK)
    label_pad = jnp.zeros((slot_total,), jnp.float32).at[block_slot].set(click_value).reshape(MEMBERS, BLK)
    live_pad = jnp.zeros((slot_total,), jnp.float32).at[block_slot].set(1.0).reshape(MEMBERS, BLK)
    coeffs = newton_blocks(padded_rows, offset, label_pad, live_pad, member_coef)
    member_value = jnp.einsum('mbk,mk->mb', padded_rows, coeffs, precision=high).reshape(slot_total)
    total_score = fixed_score + member_value[block_slot]
    return (fixed_grad, coeffs, total_score)
```

```python
import math

import jax
import jax.numpy as jnp
from jax import lax
from jax.experimental import pallas as pl
from jax.experimental.pallas import tpu as pltpu
from jax.sharding import PartitionSpec as P

MESH = pl.DeviceIdType.MESH
BLK = 64
NEWTON = 3
PAIRS = 4
f32, bf16, i32 = jnp.float32, jnp.bfloat16, jnp.int32


def iota(shape, dim):
    return lax.broadcasted_iota(i32, shape, dim)


def dot(a, b):
    return lax.dot_general(a, b, (((1,), (0,)), ((), ())), preferred_element_type=f32)


def dot_nt(a, b):
    return lax.dot_general(a, b, (((1,), (1,)), ((), ())), preferred_element_type=f32)


def split3(x):
    high = x.astype(bf16)
    rest = x - high.astype(f32)
    mid = rest.astype(bf16)
    low = (rest - mid.astype(f32)).astype(bf16)
    return high, mid, low


def stack3(x):
    return jnp.concatenate([t.astype(f32) for t in split3(x)], axis=0).astype(bf16)


def fold3(y):
    n = y.shape[0] // 3
    return (y[:n] + y[n : 2 * n]) + y[2 * n :]


def onehot(mask):
    return jnp.where(mask, 1.0, 0.0).astype(bf16)


def two_rows(x):
    return jnp.concatenate([x[0:1], x[1:2]], axis=1)


def take(x, index):
    return jnp.take_along_axis(x, index, axis=1, mode="promise_in_bounds")


def solve(rows, y):
    lane = iota((8, 128), 1)
    low = lane < 64
    col = lane & 63
    rows = list(rows)
    s = jnp.zeros((8, 128), f32)
    for q in range(0, 32, PAIRS):
        raw, vars_, offs, pivots = [], [], [], []
        for p in range(q, q + PAIRS):
            rolled = pltpu.roll(rows[p], 64, 1)
            raw += [rows[p], rows[p]]
            offs += [0, 64]
            vars_ += [p, p + 32]
            pivots += [jnp.where(low, rows[p], rolled), jnp.where(low, rolled, rows[p])]
        n = len(vars_)
        block = {
            (i, j): jnp.broadcast_to(
                raw[i][:, offs[i] + vars_[j] : offs[i] + vars_[j] + 1], (8, 128)
            )
            for i in range(n)
            for j in range(i, n)
        }
        ys = [jnp.broadcast_to(y[:, v : v + 1], (8, 128)) for v in vars_]
        half = col & 31
        inside = (half >= q) & (half < q + PAIRS)
        done = half < q + PAIRS
        t = [
            jnp.where(col == vars_[i], 1.0, jnp.where(inside, 0.0, pivots[i])) for i in range(n)
        ]
        inv, factor = [], {}
        for k in range(n):
            inv.append(1.0 / block[k, k])
            for i in range(k + 1, n):
                factor[i, k] = block[k, i] * inv[k]
            for i in range(k + 1, n):
                t[i] = t[i] - factor[i, k] * t[k]
                for j in range(i, n):
                    block[i, j] = block[i, j] - factor[i, k] * block[k, j]
        t = [t[i] * inv[i] for i in range(n)]
        for k in range(n - 1, 0, -1):
            for i in range(k):
                t[i] = t[i] - factor[k, i] * t[k]
        step = ys[0] * t[0]
        for i in range(1, n):
            step = step + ys[i] * t[i]
        s = s + jnp.where(done, step, 0.0)
        y = y - jnp.where(done, 0.0, step)
        for p in range(q + PAIRS, 32):
            pick = [jnp.where(low, off + p, off + p + 32) for off in (0, 64)]
            new = jnp.where(inside, 0.0, rows[p])
            for i in range(n):
                new = new - take(raw[i], pick[i % 2]) * t[i]
            rows[p] = new
    return s


def gram_times(gram_ref, v):
    low = iota((8, 128), 1) < 64
    total = jnp.zeros((8, 128), f32)
    for p in range(32):
        total = total + gram_ref[8 * p : 8 * p + 8, :] * take(v, jnp.where(low, p, p + 32))
    return total + pltpu.roll(total, 64, 1)


def kernel(
    coef_ref, mscore_ref, click_ref, mfeat_ref, mcoef_ref, slot_ref, feat_ref,
    grad_ref, coefs_ref, total_ref,
    fbuf, msg, rin, part, rs, own, ag, sc, scr, bk, ret, gsrc, gin,
    owner_hot, lane_of, rows_src, bhot, padded, gram,
    fsem, ssem, rsem,
):
    n_dp, n_feat = 8, 16
    n_dev = n_dp * n_feat
    dp, feat = lax.axis_index("dp"), lax.axis_index("feat")
    me = dp * n_feat + feat

    chunks = 8
    rows_chunk = fbuf.shape[0] // chunks

    def feature_copy(c):
        window = pl.ds(c * rows_chunk, rows_chunk)
        return pltpu.make_async_copy(feat_ref.at[window], fbuf.at[window], fsem.at[c])

    for c in range(chunks):
        feature_copy(c).start()

    barrier = pltpu.get_barrier_semaphore()

    def device(t):
        return (t // n_feat, lax.rem(t, n_feat))

    def others(n, body):
        def step(d, carry):
            body(d)
            return carry

        lax.fori_loop(1, n, step, 0)

    def hello(d):
        t = lax.rem(me + d, n_dev)
        pl.semaphore_signal(barrier, inc=1, device_id=device(t), device_id_type=MESH)

    others(n_dev, hello)

    def send(src, dst, which, target):
        return pltpu.make_async_remote_copy(
            src_ref=src, dst_ref=dst, send_sem=ssem.at[which], recv_sem=rsem.at[which],
            device_id=target, device_id_type=MESH,
        )

    def arrived(ref, which):
        send(ref, ref, which, (dp, feat)).wait_recv()

    def sent(ref, which):
        send(ref, ref, which, (dp, feat)).wait_send()

    slots = slot_ref[...]
    owner = slots >> 9
    own_clicks = two_rows(click_ref[pl.ds(2 * feat, 2), :])
    tag = (slots & 511) * 2 + own_clicks + 1
    hot = iota((n_dev, 256), 0) == owner
    hot_half = onehot(hot)
    before = onehot(iota((256, 256), 0) < iota((256, 256), 1))
    counts = dot(hot_half, before)
    rank = jnp.sum(jnp.where(hot, counts, 0.0), axis=0, keepdims=True).astype(i32)
    lane_row = rank + feat * 8
    owner_hot[...] = hot_half
    lane_of[...] = lane_row
    place = owner * 8 + rank
    lane_hot = iota((128, 256), 0) == lane_row

    def by_owner(row):
        return dot_nt(hot_half, jnp.where(lane_hot, row, 0.0).astype(bf16))

    tags = jnp.concatenate(
        [by_owner((tag >> 5).astype(f32)), by_owner((tag & 31).astype(f32))], axis=1
    ).astype(bf16)

    def pack(b, carry):
        base = b * 128
        sel = onehot(iota((128, 256), 0) + base == place)
        extra = onehot(iota((128, 128), 0) + base == iota((128, 128), 1) * 8 + 6)
        out = dot(sel, mfeat_ref[...]) + dot(extra, tags)
        msg[pl.ds(b * 16, 16)] = jnp.concatenate(
            [out[:, :128].reshape(16, 8, 128), out[:, 128:].reshape(16, 8, 128)], axis=1
        ).astype(bf16)
        return carry

    lax.fori_loop(0, 8, pack, 0)

    crep = jnp.broadcast_to(coef_ref[...], (128, coef_ref.shape[1])).astype(bf16)
    eye = iota((128, 128), 0) == iota((128, 128), 1)
    for c in range(chunks):
        feature_copy(c).wait()
        out = dot_nt(fbuf[c * rows_chunk : (c + 1) * rows_chunk, :], crep)
        lines = jnp.sum(jnp.where(eye, out.reshape(rows_chunk // 128, 128, 128), 0.0), axis=1)
        for j in range(rows_chunk // 256):
            part[c * (rows_chunk // 256) + j] = lines[2 * j : 2 * j + 2]

    pl.semaphore_wait(barrier, n_dev - 1)

    def send_part(d):
        f = lax.rem(feat + d, n_feat)
        send(part.at[f], rs.at[feat], 0, (dp, f)).start()

    others(n_feat, send_part)

    def send_rows(d):
        t = lax.rem(me + d, n_dev)
        send(msg.at[t], rin.at[me], 1, device(t)).start()

    others(n_dev, send_rows)
    rs[feat] = part[feat]
    rin[me] = msg[me]

    arrived(rs.at[pl.ds(0, n_feat - 1)], 0)
    score = rs[0]
    for f in range(1, n_feat):
        score = score + rs[f]
    own[...] = score
    ag[feat] = score
    own_row = two_rows(score)
    lane_hot = iota((128, 256), 0) == lane_of[...]
    parts = [
        dot_nt(owner_hot[...], jnp.where(lane_hot, t.astype(f32), 0.0).astype(bf16))
        for t in split3(own_row)
    ]
    by = (parts[0] + parts[1]) + parts[2]
    sc[...] = by.reshape(n_dev, 1, 128)

    def send_score(d):
        t = lax.rem(me + d, n_dev)
        send(sc.at[t], scr.at[me], 2, device(t)).start()

    others(n_dev, send_score)

    def send_own(d):
        f = lax.rem(feat + d, n_feat)
        send(own, ag.at[feat], 3, (dp, f)).start()

    others(n_feat, send_own)
    scr[me] = sc[me]

    arrived(rin.at[pl.ds(0, n_dev - 1)], 1)

    def unpack(b, carry):
        got = rin[pl.ds(b * 16, 16)].astype(f32)
        rows_src[pl.ds(b * 128, 128), :] = jnp.concatenate(
            [got[:, 0:8].reshape(128, 128), got[:, 8:16].reshape(128, 128)], axis=1
        ).astype(bf16)
        return carry

    lax.fori_loop(0, 8, unpack, 0)
    src = iota((8, 1024), 1)
    tag_sel = onehot(((src & 7) == 6) & ((src >> 7) == iota((8, 1024), 0)))
    tags_in = dot(tag_sel, rows_src[...])
    tag_in = (tags_in[:, :128] * 32.0 + tags_in[:, 128:]).astype(i32) - 1
    used = tag_in >= 0
    slot_in = jnp.where(used, tag_in >> 1, -1)
    label_in = jnp.where(used, tag_in & 1, 0)

    def line(x):
        return jnp.concatenate([x[a : a + 1] for a in range(8)], axis=1)

    slot_line = line(slot_in)
    member_line = slot_line >> 6
    spot_line = jnp.where(slot_line < 0, -1, slot_line & 63)
    mine = iota((8, 1024), 0) == member_line
    bhot[...] = onehot((iota((128, 1024), 0) & 63) == spot_line)

    for h in range(4):
        sel = onehot(iota((128, 1024), 0) + 128 * h == slot_line)
        padded[128 * h : 128 * h + 128, :] = dot(sel, rows_src[...]).astype(bf16)

    low = iota((32, 128), 1) < 64
    for h in range(4):
        pair = padded[128 * h : 128 * h + 128, :]
        prod = dot_nt(pair, pair)
        turned = pltpu.roll(prod, 64, 1)
        gram[pl.ds(2 * h, 32, stride=8), :] = jnp.where(low, prod[0:32], turned[32:64])
        gram[pl.ds(2 * h + 1, 32, stride=8), :] = jnp.where(low, turned[64:96], prod[96:128])

    marks = jnp.concatenate(
        [jnp.where(mine, line(label_in).astype(f32), 0.0), jnp.where(mine, 1.0, 0.0)], axis=0
    ).astype(bf16)
    marked = dot_nt(marks, bhot[...])
    label, live = marked[0:8], marked[8:16]

    member_of = iota((8, 512), 1) >> 6 == iota((8, 512), 0)
    first = jnp.where(member_of, fold3(dot_nt(stack3(mcoef_ref[...]), padded[...])), 0.0)
    first = (first[:, 0:128] + first[:, 128:256]) + (first[:, 256:384] + first[:, 384:512])
    start = first + pltpu.roll(first, 64, 1)

    arrived(ag.at[pl.ds(0, n_feat - 1)], 3)
    scores = jnp.concatenate([ag[f] for f in range(n_feat)], axis=0)
    resid = jax.nn.sigmoid(scores + mscore_ref[...]) - click_ref[...].astype(f32)
    grad = jnp.zeros((8, grad_ref.shape[1]), f32)
    for b in range(4):
        eight = resid[8 * b : 8 * b + 8]
        wide = jnp.concatenate([eight] * 8, axis=1)
        wide = jnp.where(iota((8, 1024), 1) >> 7 == iota((8, 1024), 0), wide, 0.0).astype(bf16)
        grad = grad + dot(wide, fbuf[1024 * b : 1024 * b + 1024, :])
    gsrc[...] = jnp.sum(grad, axis=0, keepdims=True)

    def send_grad(d):
        t = lax.rem(dp + d, n_dp)
        send(gsrc, gin.at[dp], 4, (t, feat)).start()

    others(n_dp, send_grad)
    gin[dp] = gsrc[...]

    arrived(scr.at[pl.ds(0, n_dev - 1)], 2)
    score_in = [jnp.sum(scr[16 * a : 16 * a + 16], axis=0) for a in range(8)]
    score_line = jnp.concatenate(score_in, axis=1)
    offset = fold3(dot_nt(stack3(jnp.where(mine, score_line, 0.0)), bhot[...]))

    lane = iota((8, 128), 1)
    low = lane < 64

    def newton(step, carry):
        u, _ = carry
        prob = jax.nn.sigmoid(offset + u)
        slope = live * (prob - label)
        root = jnp.sqrt(live * prob * (1.0 - prob))
        rhs = root * (gram_times(gram, slope) + u)
        rows = []
        for p in range(32):
            scaled = gram[8 * p : 8 * p + 8, :] * root * take(root, jnp.where(low, p, p + 32))
            diagonal = (lane == p) | (lane == p + 96)
            rows.append(scaled + jnp.where(diagonal, 1.0, 0.0))
        beta = root * solve(rows, rhs) - slope
        return gram_times(gram, beta), beta

    value, beta = lax.fori_loop(0, NEWTON, newton, (start, jnp.zeros((8, 128), f32)))

    back = fold3(dot(stack3(jnp.where(low, value, 0.0)), bhot[...]))
    back = jnp.sum(jnp.where(mine, back, 0.0), axis=0, keepdims=True)
    for a in range(8):
        bk[a] = back[:, 128 * a : 128 * a + 128]

    def send_back(d):
        t = lax.rem(me + d, n_dev)
        send(bk.at[t // n_feat], ret.at[me], 5, device(t)).start()

    others(n_dev, send_back)
    ret[me] = bk[dp]

    spread = jnp.where(member_of, jnp.concatenate([beta] * 4, axis=1), 0.0)
    coefs_ref[...] = fold3(dot(stack3(spread), padded[...]))

    arrived(gin.at[pl.ds(0, n_dp - 1)], 4)
    full = gin[0]
    for t in range(1, n_dp):
        full = full + gin[t]
    grad_ref[...] = full / math.sqrt(n_dev * 256)

    sent(part.at[pl.ds(0, n_feat - 1)], 0)
    sent(msg.at[pl.ds(0, n_dev - 1)], 1)
    sent(sc.at[pl.ds(0, n_dev - 1)], 2)
    sent(ag.at[pl.ds(0, n_feat - 1)], 3)
    sent(gin.at[pl.ds(0, n_dp - 1)], 4)

    arrived(ret.at[pl.ds(0, n_dev - 1)], 5)
    lane_half = onehot(iota((128, 256), 0) == lane_of[...])
    came = ret[...].reshape(n_dev, 128)
    got = [dot(t, lane_half) for t in split3(came)]
    got = (got[0] + got[1]) + got[2]
    mine_back = jnp.sum(jnp.where(iota((n_dev, 256), 0) == slot_ref[...] >> 9, got, 0.0), axis=0)
    total_ref[...] = two_rows(own[...]) + mine_back[None, :]
    sent(ret.at[pl.ds(0, n_dev - 1)], 5)


def per_device(
    features, fixed_coef, member_score, clicks, member_features, member_coef, block_slot
):
    n_dev = 128
    rows, width = features.shape
    vmem = pl.BlockSpec(memory_space=pltpu.VMEM)
    grad, coefs, total = pl.pallas_call(
        kernel,
        name="glmix",
        out_shape=(
            jax.ShapeDtypeStruct((1, width), f32),
            jax.ShapeDtypeStruct(member_coef.shape, f32),
            jax.ShapeDtypeStruct((1, block_slot.shape[0]), f32),
        ),
        in_specs=[vmem] * 6 + [pl.BlockSpec(memory_space=pl.ANY)],
        out_specs=(vmem,) * 3,
        scratch_shapes=[
            pltpu.VMEM((rows, width), bf16),
            pltpu.VMEM((n_dev, 16, 128), bf16),
            pltpu.VMEM((n_dev, 16, 128), bf16),
            pltpu.VMEM((16, 2, 128), f32),
            pltpu.VMEM((16, 2, 128), f32),
            pltpu.VMEM((2, 128), f32),
            pltpu.VMEM((16, 2, 128), f32),
            pltpu.VMEM((n_dev, 1, 128), f32),
            pltpu.VMEM((n_dev, 1, 128), f32),
            pltpu.VMEM((8, 1, 128), f32),
            pltpu.VMEM((n_dev, 1, 128), f32),
            pltpu.VMEM((1, width), f32),
            pltpu.VMEM((8, 1, width), f32),
            pltpu.VMEM((n_dev, 256), bf16),
            pltpu.VMEM((1, 256), i32),
            pltpu.VMEM((1024, 256), bf16),
            pltpu.VMEM((128, 1024), bf16),
            pltpu.VMEM((512, 256), bf16),
            pltpu.VMEM((256, 128), f32),
            pltpu.SemaphoreType.DMA((8,)),
            pltpu.SemaphoreType.DMA((6,)),
            pltpu.SemaphoreType.DMA((6,)),
        ],
        compiler_params=pltpu.CompilerParams(collective_id=0, has_side_effects=True),
    )(
        fixed_coef.reshape(1, width),
        member_score.reshape(rows // 128, 128),
        clicks.reshape(rows // 128, 128),
        member_features,
        member_coef,
        block_slot.reshape(1, -1),
        features,
    )
    return grad.reshape(-1), coefs, total.reshape(-1)


def solution(mesh):
    return jax.shard_map(
        per_device,
        mesh=mesh,
        in_specs=(
            P("dp", "feat"),
            P("feat"),
            P("dp"),
            P("dp"),
            P(("dp", "feat"), None),
            P(("dp", "feat"), None),
            P(("dp", "feat")),
        ),
        out_specs=(P("feat"), P(("dp", "feat"), None), P(("dp", "feat"))),
        check_vma=False,
    )
```

```python
import math

import jax
import jax.numpy as jnp
from jax import lax
from jax.experimental import pallas as pl
from jax.experimental.pallas import tpu as pltpu
from jax.sharding import PartitionSpec as P

SPLIT = 84
LOGICAL = pl.DeviceIdType.LOGICAL
BLK = 64
NEWTON = 3
PAIRS = 4
f32, bf16, i32 = jnp.float32, jnp.bfloat16, jnp.int32


def iota(shape, dim):
    return lax.broadcasted_iota(i32, shape, dim)


def dot(a, b):
    return lax.dot_general(a, b, (((1,), (0,)), ((), ())), preferred_element_type=f32)


def dot_nt(a, b):
    return lax.dot_general(a, b, (((1,), (1,)), ((), ())), preferred_element_type=f32)


def split3(x):
    high = x.astype(bf16)
    rest = x - high.astype(f32)
    mid = rest.astype(bf16)
    low = (rest - mid.astype(f32)).astype(bf16)
    return high, mid, low


def stack3(x):
    return jnp.concatenate([t.astype(f32) for t in split3(x)], axis=0).astype(bf16)


def fold3(y):
    n = y.shape[0] // 3
    return (y[:n] + y[n : 2 * n]) + y[2 * n :]


def onehot(mask):
    return jnp.where(mask, 1.0, 0.0).astype(bf16)


def two_rows(x):
    return jnp.concatenate([x[0:1], x[1:2]], axis=1)


def take(x, index):
    return jnp.take_along_axis(x, index, axis=1, mode="promise_in_bounds")


def solve(rows, y):
    lane = iota((8, 128), 1)
    low = lane < 64
    col = lane & 63
    rows = list(rows)
    s = jnp.zeros((8, 128), f32)
    for q in range(0, 32, PAIRS):
        raw, vars_, offs, pivots = [], [], [], []
        for p in range(q, q + PAIRS):
            rolled = pltpu.roll(rows[p], 64, 1)
            raw += [rows[p], rows[p]]
            offs += [0, 64]
            vars_ += [p, p + 32]
            pivots += [jnp.where(low, rows[p], rolled), jnp.where(low, rolled, rows[p])]
        n = len(vars_)
        block = {
            (i, j): jnp.broadcast_to(
                raw[i][:, offs[i] + vars_[j] : offs[i] + vars_[j] + 1], (8, 128)
            )
            for i in range(n)
            for j in range(i, n)
        }
        ys = [jnp.broadcast_to(y[:, v : v + 1], (8, 128)) for v in vars_]
        half = col & 31
        inside = (half >= q) & (half < q + PAIRS)
        done = half < q + PAIRS
        t = [
            jnp.where(col == vars_[i], 1.0, jnp.where(inside, 0.0, pivots[i])) for i in range(n)
        ]
        inv, factor = [], {}
        for k in range(n):
            inv.append(1.0 / block[k, k])
            for i in range(k + 1, n):
                factor[i, k] = block[k, i] * inv[k]
            for i in range(k + 1, n):
                t[i] = t[i] - factor[i, k] * t[k]
                for j in range(i, n):
                    block[i, j] = block[i, j] - factor[i, k] * block[k, j]
        t = [t[i] * inv[i] for i in range(n)]
        for k in range(n - 1, 0, -1):
            for i in range(k):
                t[i] = t[i] - factor[k, i] * t[k]
        step = ys[0] * t[0]
        for i in range(1, n):
            step = step + ys[i] * t[i]
        s = s + jnp.where(done, step, 0.0)
        y = y - jnp.where(done, 0.0, step)
        for p in range(q + PAIRS, 32):
            pick = [jnp.where(low, off + p, off + p + 32) for off in (0, 64)]
            new = jnp.where(inside, 0.0, rows[p])
            for i in range(n):
                new = new - take(raw[i], pick[i % 2]) * t[i]
            rows[p] = new
    return s


def gram_times(gram_ref, v):
    low = iota((8, 128), 1) < 64
    total = jnp.zeros((8, 128), f32)
    for p in range(32):
        total = total + gram_ref[8 * p : 8 * p + 8, :] * take(v, jnp.where(low, p, p + 32))
    return total + pltpu.roll(total, 64, 1)


def kernel(
    coef_hbm, mscore_hbm, click_hbm, mfeat_hbm, mcoef_hbm, slot_hbm, feat_ref,
    out_ref,
    coef_ref, mscore_ref, click_ref, mfeat_ref, mcoef_ref, slot_ref,
    fbuf, msg, rin, part, rs, own, ag, sc, scr, bk, ret, gsrc, gin,
    owner_hot, lane_of, rows_src, bhot, padded, gram,
    isem, fsem, ssem, rsem,
):
    n_dp, n_feat = 8, 16
    n_dev = n_dp * n_feat
    dp, feat = lax.axis_index("dp"), lax.axis_index("feat")
    me = dp * n_feat + feat

    chunks = 8
    rows_chunk = fbuf.shape[0] // chunks

    def feature_copy(c):
        window = pl.ds(c * rows_chunk, rows_chunk)
        return pltpu.make_async_copy(feat_ref.at[window], fbuf.at[window], fsem.at[c])

    loads = [
        pltpu.make_async_copy(src, dst, isem.at[i])
        for i, (src, dst) in enumerate([
            (slot_hbm, slot_ref), (click_hbm, click_ref), (mfeat_hbm, mfeat_ref),
            (coef_hbm, coef_ref), (mscore_hbm, mscore_ref), (mcoef_hbm, mcoef_ref),
        ])
    ]
    for load in loads:
        load.start()
    for c in range(chunks):
        feature_copy(c).start()

    barrier = pltpu.get_barrier_semaphore()

    dps = [2 * lax.rem(dp // 2 + dy, 4) + lax.rem(dp + dc, 2) for dy in range(4) for dc in range(2)]
    feats = [
        4 * lax.rem(feat // 4 + dz, 4) + lax.rem(feat + dx, 4) for dz in range(4) for dx in range(4)
    ]
    hops = [0, 1, 2, 1]
    dp_far = sorted(range(1, 8), key=lambda a: -hops[a // 2])
    feat_far = sorted(range(1, 16), key=lambda b: -hops[b // 4] - hops[b % 4])
    all_far = sorted(
        ((a, b) for a in range(8) for b in range(16) if a or b),
        key=lambda ab: -hops[ab[0] // 2] - hops[ab[1] // 4] - hops[ab[1] % 4],
    )

    for a, b in all_far:
        pl.semaphore_signal(
            barrier, inc=1, device_id=dps[a] * n_feat + feats[b], device_id_type=LOGICAL
        )

    def send(src, dst, which, target):
        return pltpu.make_async_remote_copy(
            src_ref=src, dst_ref=dst, send_sem=ssem.at[which], recv_sem=rsem.at[which],
            device_id=target, device_id_type=LOGICAL,
        )

    def arrived(ref, which):
        send(ref, ref, which, me).wait_recv()

    def sent(ref, which):
        send(ref, ref, which, me).wait_send()

    for load in loads:
        load.wait()
    slots = slot_ref[...]
    owner = slots >> 9
    own_clicks = two_rows(click_ref[pl.ds(2 * feat, 2), :])
    tag = (slots & 511) * 2 + own_clicks + 1
    hot = iota((n_dev, 256), 0) == owner
    hot_half = onehot(hot)
    before = onehot(iota((256, 256), 0) < iota((256, 256), 1))
    counts = dot(hot_half, before)
    rank = jnp.sum(jnp.where(hot, counts, 0.0), axis=0, keepdims=True).astype(i32)
    lane_row = rank + feat * 8
    owner_hot[...] = hot_half
    lane_of[...] = lane_row
    place = owner * 8 + rank
    lane_hot = iota((128, 256), 0) == lane_row

    def by_owner(row):
        return dot_nt(hot_half, jnp.where(lane_hot, row, 0.0).astype(bf16))

    tags = jnp.concatenate(
        [by_owner((tag >> 5).astype(f32)), by_owner((tag & 31).astype(f32))], axis=1
    ).astype(bf16)

    def pack(b, carry):
        base = b * 128
        sel = onehot(iota((128, 256), 0) + base == place)
        extra = onehot(iota((128, 128), 0) + base == iota((128, 128), 1) * 8 + 6)
        out = dot(sel, mfeat_ref[...]) + dot(extra, tags)
        msg[pl.ds(b * 16, 16)] = jnp.concatenate(
            [out[:, :128].reshape(16, 8, 128), out[:, 128:].reshape(16, 8, 128)], axis=1
        ).astype(bf16)
        return carry

    lax.fori_loop(0, 8, pack, 0)

    coef = jnp.broadcast_to(coef_ref[...], (8, coef_ref.shape[1])).astype(bf16)
    for c in range(chunks):
        feature_copy(c).wait()
        out = dot_nt(coef, fbuf[c * rows_chunk : (c + 1) * rows_chunk, :])[0:1]
        for j in range(rows_chunk // 256):
            part[c * (rows_chunk // 256) + j] = out[:, 256 * j : 256 * j + 256]

    pl.semaphore_wait(barrier, n_dev - 1)

    for b in feat_far:
        send(part.at[feats[b]], rs.at[feat], 0, dp * n_feat + feats[b]).start()

    for a, b in all_far[:SPLIT]:
        t = dps[a] * n_feat + feats[b]
        send(msg.at[t], rin.at[me], 1, t).start()

    rs[feat] = part[feat]
    rin[me] = msg[me]

    arrived(rs.at[pl.ds(0, n_feat - 1)], 0)
    score = rs[0]
    for f in range(1, n_feat):
        score = score + rs[f]
    own[...] = score
    ag[feat] = score
    lane_hot = iota((128, 256), 0) == lane_of[...]
    parts = [
        dot_nt(owner_hot[...], jnp.where(lane_hot, t.astype(f32), 0.0).astype(bf16))
        for t in split3(score)
    ]
    by = (parts[0] + parts[1]) + parts[2]
    sc[...] = by.reshape(n_dev, 1, 128)

    for a, b in all_far:
        t = dps[a] * n_feat + feats[b]
        send(sc.at[t], scr.at[me], 2, t).start()

    for a, b in all_far[SPLIT:]:
        t = dps[a] * n_feat + feats[b]
        send(msg.at[t], rin.at[me], 1, t).start()

    for b in feat_far:
        send(own, ag.at[feat], 3, dp * n_feat + feats[b]).start()

    scr[me] = sc[me]

    arrived(rin.at[pl.ds(0, n_dev - 1)], 1)

    def unpack(b, carry):
        got = rin[pl.ds(b * 16, 16)].astype(f32)
        rows_src[pl.ds(b * 128, 128), :] = jnp.concatenate(
            [got[:, 0:8].reshape(128, 128), got[:, 8:16].reshape(128, 128)], axis=1
        ).astype(bf16)
        return carry

    lax.fori_loop(0, 8, unpack, 0)
    src = iota((8, 1024), 1)
    tag_sel = onehot(((src & 7) == 6) & ((src >> 7) == iota((8, 1024), 0)))
    tags_in = dot(tag_sel, rows_src[...])
    tag_in = (tags_in[:, :128] * 32.0 + tags_in[:, 128:]).astype(i32) - 1
    used = tag_in >= 0
    slot_in = jnp.where(used, tag_in >> 1, -1)
    label_in = jnp.where(used, tag_in & 1, 0)

    def line(x):
        return jnp.concatenate([x[a : a + 1] for a in range(8)], axis=1)

    slot_line = line(slot_in)
    member_line = slot_line >> 6
    spot_line = jnp.where(slot_line < 0, -1, slot_line & 63)
    mine = iota((8, 1024), 0) == member_line
    bhot[...] = onehot((iota((128, 1024), 0) & 63) == spot_line)

    for h in range(4):
        sel = onehot(iota((128, 1024), 0) + 128 * h == slot_line)
        padded[128 * h : 128 * h + 128, :] = dot(sel, rows_src[...]).astype(bf16)

    low = iota((32, 128), 1) < 64
    for h in range(4):
        pair = padded[128 * h : 128 * h + 128, :]
        prod = dot_nt(pair, pair)
        turned = pltpu.roll(prod, 64, 1)
        gram[pl.ds(2 * h, 32, stride=8), :] = jnp.where(low, prod[0:32], turned[32:64])
        gram[pl.ds(2 * h + 1, 32, stride=8), :] = jnp.where(low, turned[64:96], prod[96:128])

    marks = jnp.concatenate(
        [jnp.where(mine, line(label_in).astype(f32), 0.0), jnp.where(mine, 1.0, 0.0)], axis=0
    ).astype(bf16)
    marked = dot_nt(marks, bhot[...])
    label, live = marked[0:8], marked[8:16]

    member_of = iota((8, 512), 1) >> 6 == iota((8, 512), 0)
    first = jnp.where(member_of, fold3(dot_nt(stack3(mcoef_ref[...]), padded[...])), 0.0)
    first = (first[:, 0:128] + first[:, 128:256]) + (first[:, 256:384] + first[:, 384:512])
    start = first + pltpu.roll(first, 64, 1)

    arrived(scr.at[pl.ds(0, n_dev - 1)], 2)
    score_in = [jnp.sum(scr[16 * a : 16 * a + 16], axis=0) for a in range(8)]
    score_line = jnp.concatenate(score_in, axis=1)
    offset = fold3(dot_nt(stack3(jnp.where(mine, score_line, 0.0)), bhot[...]))

    lane = iota((8, 128), 1)
    low = lane < 64

    def newton(step, carry):
        u, _ = carry
        prob = jax.nn.sigmoid(offset + u)
        slope = live * (prob - label)
        root = jnp.sqrt(live * prob * (1.0 - prob))
        rhs = root * (gram_times(gram, slope) + u)
        rows = []
        for p in range(32):
            scaled = gram[8 * p : 8 * p + 8, :] * root * take(root, jnp.where(low, p, p + 32))
            diagonal = (lane == p) | (lane == p + 96)
            rows.append(scaled + jnp.where(diagonal, 1.0, 0.0))
        beta = root * solve(rows, rhs) - slope
        return gram_times(gram, beta), beta

    value, beta = lax.fori_loop(0, NEWTON, newton, (start, jnp.zeros((8, 128), f32)))

    back = fold3(dot(stack3(jnp.where(low, value, 0.0)), bhot[...]))
    back = jnp.sum(jnp.where(mine, back, 0.0), axis=0, keepdims=True)
    for a in range(8):
        bk[a] = back[:, 128 * a : 128 * a + 128]

    for a, b in all_far:
        send(bk.at[dps[a]], ret.at[me], 5, dps[a] * n_feat + feats[b]).start()

    ret[me] = bk[dp]

    arrived(ag.at[pl.ds(0, n_feat - 1)], 3)
    scores = jnp.concatenate(
        [ag[f][:, 128 * h : 128 * h + 128] for f in range(n_feat) for h in range(2)], axis=0
    )
    resid = jax.nn.sigmoid(scores + mscore_ref[...]) - click_ref[...].astype(f32)
    grad = jnp.zeros((8, fbuf.shape[1]), f32)
    for b in range(4):
        eight = resid[8 * b : 8 * b + 8]
        wide = jnp.concatenate([eight] * 8, axis=1)
        wide = jnp.where(iota((8, 1024), 1) >> 7 == iota((8, 1024), 0), wide, 0.0).astype(bf16)
        grad = grad + dot(wide, fbuf[1024 * b : 1024 * b + 1024, :])
    gsrc[...] = jnp.sum(grad, axis=0, keepdims=True)

    for a in dp_far:
        send(gsrc, gin.at[dp], 4, dps[a] * n_feat + feat).start()

    gin[dp] = gsrc[...]

    spread = jnp.where(member_of, jnp.concatenate([beta] * 4, axis=1), 0.0)
    out_ref[0:8, :] = fold3(dot(stack3(spread), padded[...]))

    arrived(gin.at[pl.ds(0, n_dp - 1)], 4)
    full = gin[0]
    for t in range(1, n_dp):
        full = full + gin[t]
    full = full / math.sqrt(n_dev * 256)
    out_ref[8:9, :] = full[:, :256]
    out_ref[9:10, :] = full[:, 256:]

    sent(part.at[pl.ds(0, n_feat - 1)], 0)
    sent(msg.at[pl.ds(0, n_dev - 1)], 1)
    sent(sc.at[pl.ds(0, n_dev - 1)], 2)
    sent(ag.at[pl.ds(0, n_feat - 1)], 3)
    sent(gin.at[pl.ds(0, n_dp - 1)], 4)

    arrived(ret.at[pl.ds(0, n_dev - 1)], 5)
    lane_half = onehot(iota((128, 256), 0) == lane_of[...])
    came = ret[...].reshape(n_dev, 128)
    got = [dot(t, lane_half) for t in split3(came)]
    got = (got[0] + got[1]) + got[2]
    mine_back = jnp.sum(jnp.where(iota((n_dev, 256), 0) == slot_ref[...] >> 9, got, 0.0), axis=0)
    out_ref[10:11, :] = own[...] + mine_back[None, :]
    sent(ret.at[pl.ds(0, n_dev - 1)], 5)


def split(merged_ref, grad_ref, coefs_ref, total_ref):
    coefs_ref[...] = merged_ref[0:8, :]
    grad_ref[...] = jnp.concatenate([merged_ref[8:9, :], merged_ref[9:10, :]], axis=1)
    total_ref[...] = merged_ref[10:11, :]


def per_device(
    features, fixed_coef, member_score, clicks, member_features, member_coef, block_slot
):
    n_dev = 128
    rows, width = features.shape
    vmem = pl.BlockSpec(memory_space=pltpu.VMEM)
    merged = pl.pallas_call(
        kernel,
        name="glmix",
        out_shape=jax.ShapeDtypeStruct((16, 256), f32),
        in_specs=[pl.BlockSpec(memory_space=pl.ANY)] * 7,
        out_specs=vmem,
        scratch_shapes=[
            pltpu.VMEM((1, width), f32),
            pltpu.VMEM((rows // 128, 128), f32),
            pltpu.VMEM((rows // 128, 128), i32),
            pltpu.VMEM(member_features.shape, bf16),
            pltpu.VMEM(member_coef.shape, f32),
            pltpu.VMEM((1, 256), i32),
            pltpu.VMEM((rows, width), bf16),
            pltpu.VMEM((n_dev, 16, 128), bf16),
            pltpu.VMEM((n_dev, 16, 128), bf16),
            pltpu.VMEM((16, 1, 256), f32),
            pltpu.VMEM((16, 1, 256), f32),
            pltpu.VMEM((1, 256), f32),
            pltpu.VMEM((16, 1, 256), f32),
            pltpu.VMEM((n_dev, 1, 128), f32),
            pltpu.VMEM((n_dev, 1, 128), f32),
            pltpu.VMEM((8, 1, 128), f32),
            pltpu.VMEM((n_dev, 1, 128), f32),
            pltpu.VMEM((1, width), f32),
            pltpu.VMEM((8, 1, width), f32),
            pltpu.VMEM((n_dev, 256), bf16),
            pltpu.VMEM((1, 256), i32),
            pltpu.VMEM((1024, 256), bf16),
            pltpu.VMEM((128, 1024), bf16),
            pltpu.VMEM((512, 256), bf16),
            pltpu.VMEM((256, 128), f32),
            pltpu.SemaphoreType.DMA((6,)),
            pltpu.SemaphoreType.DMA((8,)),
            pltpu.SemaphoreType.DMA((6,)),
            pltpu.SemaphoreType.DMA((6,)),
        ],
        compiler_params=pltpu.CompilerParams(collective_id=0, has_side_effects=True),
    )(
        fixed_coef.reshape(1, width),
        member_score.reshape(rows // 128, 128),
        clicks.reshape(rows // 128, 128),
        member_features,
        member_coef,
        block_slot.reshape(1, -1),
        features,
    )
    grad, coefs, total = pl.pallas_call(
        split,
        name="split",
        out_shape=(
            jax.ShapeDtypeStruct((1, width), f32),
            jax.ShapeDtypeStruct(member_coef.shape, f32),
            jax.ShapeDtypeStruct((1, block_slot.shape[0]), f32),
        ),
        in_specs=[vmem],
        out_specs=(vmem,) * 3,
    )(merged)
    return grad.reshape(-1), coefs, total.reshape(-1)


def solution(mesh):
    return jax.shard_map(
        per_device,
        mesh=mesh,
        in_specs=(
            P("dp", "feat"),
            P("feat"),
            P("dp"),
            P("dp"),
            P(("dp", "feat"), None),
            P(("dp", "feat"), None),
            P(("dp", "feat")),
        ),
        out_specs=(P("feat"), P(("dp", "feat"), None), P(("dp", "feat"))),
        check_vma=False,
    )
```

```python
import math

import jax
import jax.numpy as jnp
from jax import lax
from jax.experimental import pallas as pl
from jax.experimental.pallas import tpu as pltpu
from jax.sharding import PartitionSpec as P

SPLIT = 84
LOGICAL = pl.DeviceIdType.LOGICAL
BLK = 64
NEWTON = 3
PAIRS = 4
f32, bf16, i32 = jnp.float32, jnp.bfloat16, jnp.int32


def iota(shape, dim):
    return lax.broadcasted_iota(i32, shape, dim)


def dot(a, b):
    return lax.dot_general(a, b, (((1,), (0,)), ((), ())), preferred_element_type=f32)


def dot_nt(a, b):
    return lax.dot_general(a, b, (((1,), (1,)), ((), ())), preferred_element_type=f32)


def split3(x):
    high = x.astype(bf16)
    rest = x - high.astype(f32)
    mid = rest.astype(bf16)
    low = (rest - mid.astype(f32)).astype(bf16)
    return high, mid, low


def stack3(x):
    return jnp.concatenate([t.astype(f32) for t in split3(x)], axis=0).astype(bf16)


def fold3(y):
    n = y.shape[0] // 3
    return (y[:n] + y[n : 2 * n]) + y[2 * n :]


def onehot(mask):
    return jnp.where(mask, 1.0, 0.0).astype(bf16)


def two_rows(x):
    return jnp.concatenate([x[0:1], x[1:2]], axis=1)


def take(x, index):
    return jnp.take_along_axis(x, index, axis=1, mode="promise_in_bounds")


def solve(rows, y):
    lane = iota((8, 128), 1)
    low = lane < 64
    col = lane & 63
    half = lane & 31
    rows = list(rows)
    s = jnp.zeros((8, 128), f32)
    for q in range(0, 32, PAIRS):
        unknowns = [b + p for b in (0, 32) for p in range(q, q + PAIRS)]
        n = len(unknowns)
        sides = [jnp.where(low, v, v + 64) for v in unknowns]
        block = {}
        for j, v in enumerate(unknowns):
            for i in range(min(j + 1, PAIRS)):
                block[i, j] = jnp.broadcast_to(rows[q + i][:, v : v + 1], (8, 128))
            for i in range(PAIRS, j + 1):
                block[i, j] = jnp.broadcast_to(rows[q + i - PAIRS][:, v + 64 : v + 65], (8, 128))
        ys = [jnp.broadcast_to(y[:, v : v + 1], (8, 128)) for v in unknowns]
        rolled = [pltpu.roll(rows[p], 64, 1) for p in range(q, q + PAIRS)]
        pivots = [jnp.where(low, rows[q + i], rolled[i]) for i in range(PAIRS)]
        pivots += [jnp.where(low, rolled[i], rows[q + i]) for i in range(PAIRS)]
        inside = (half >= q) & (half < q + PAIRS)
        done = half < q + PAIRS
        t = [
            jnp.where(col == unknowns[i], 1.0, jnp.where(inside, 0.0, pivots[i])) for i in range(n)
        ]
        invs, factor = {}, {}
        for k in range(0, n, 2):
            a, b, c = block[k, k], block[k, k + 1], block[k + 1, k + 1]
            scale = 1.0 / (a * c - b * b)
            invs[k] = (c * scale, b * scale, a * scale)
            for i in range(k + 2, n):
                factor[i, k] = (c * block[k, i] - b * block[k + 1, i]) * scale
                factor[i, k + 1] = (a * block[k + 1, i] - b * block[k, i]) * scale
            for i in range(k + 2, n):
                t[i] = t[i] - (factor[i, k] * t[k] + factor[i, k + 1] * t[k + 1])
                for j in range(i, n):
                    block[i, j] = block[i, j] - (
                        factor[i, k] * block[k, j] + factor[i, k + 1] * block[k + 1, j]
                    )
        for k in range(0, n, 2):
            a, b, c = invs[k]
            t[k], t[k + 1] = a * t[k] - b * t[k + 1], c * t[k + 1] - b * t[k]
        for k in range(n - 2, 0, -2):
            for i in range(k):
                t[i] = t[i] - (factor[k, i] * t[k] + factor[k + 1, i] * t[k + 1])
        step = tree_sum([ys[i] * t[i] for i in range(n)])
        s = s + jnp.where(done, step, 0.0)
        y = y - jnp.where(done, 0.0, step)
        for group in (range(q + PAIRS, min(q + 2 * PAIRS, 32)), range(q + 2 * PAIRS, 32)):
            terms = [[take(rows[p], sides[i]) * t[i] for p in group] for i in range(n)]
            for j, p in enumerate(group):
                change = tree_sum([terms[i][j] for i in range(n)])
                rows[p] = jnp.where(inside, 0.0, rows[p]) - change
    return s


def tree_sum(terms):
    while len(terms) > 1:
        terms = [sum(terms[i + 1 : i + 2], terms[i]) for i in range(0, len(terms), 2)]
    return terms[0]


def gram_times(gram_ref, v):
    low = iota((8, 128), 1) < 64
    total = tree_sum(
        [gram_ref[8 * p : 8 * p + 8, :] * take(v, jnp.where(low, p, p + 32)) for p in range(32)]
    )
    return total + pltpu.roll(total, 64, 1)


def kernel(
    coef_hbm, mscore_hbm, click_hbm, mfeat_hbm, mcoef_hbm, slot_hbm, feat_ref,
    out_ref,
    coef_ref, mscore_ref, click_ref, mfeat_ref, mcoef_ref, slot_ref,
    fbuf, msg, rin, part, rs, own, ag, sc, scr, bk, ret, gsrc, gin,
    owner_hot, lane_of, rows_src, bhot, padded, gram,
    isem, fsem, ssem, rsem,
):
    n_dp, n_feat = 8, 16
    n_dev = n_dp * n_feat
    dp, feat = lax.axis_index("dp"), lax.axis_index("feat")
    me = dp * n_feat + feat

    chunks = 8
    rows_chunk = fbuf.shape[0] // chunks

    def feature_copy(c):
        window = pl.ds(c * rows_chunk, rows_chunk)
        return pltpu.make_async_copy(feat_ref.at[window], fbuf.at[window], fsem.at[c])

    loads = [
        pltpu.make_async_copy(src, dst, isem.at[i])
        for i, (src, dst) in enumerate([
            (slot_hbm, slot_ref), (click_hbm, click_ref), (mfeat_hbm, mfeat_ref),
            (coef_hbm, coef_ref), (mscore_hbm, mscore_ref), (mcoef_hbm, mcoef_ref),
        ])
    ]
    for load in loads:
        load.start()
    for c in range(chunks):
        feature_copy(c).start()

    barrier = pltpu.get_barrier_semaphore()

    dps = [2 * lax.rem(dp // 2 + dy, 4) + lax.rem(dp + dc, 2) for dy in range(4) for dc in range(2)]
    feats = [
        4 * lax.rem(feat // 4 + dz, 4) + lax.rem(feat + dx, 4) for dz in range(4) for dx in range(4)
    ]
    hops = [0, 1, 2, 1]
    dp_far = sorted(range(1, 8), key=lambda a: -hops[a // 2])
    feat_far = sorted(range(1, 16), key=lambda b: -hops[b // 4] - hops[b % 4])
    all_far = sorted(
        ((a, b) for a in range(8) for b in range(16) if a or b),
        key=lambda ab: -hops[ab[0] // 2] - hops[ab[1] // 4] - hops[ab[1] % 4],
    )

    for a, b in all_far:
        pl.semaphore_signal(
            barrier, inc=1, device_id=dps[a] * n_feat + feats[b], device_id_type=LOGICAL
        )

    def send(src, dst, which, target):
        return pltpu.make_async_remote_copy(
            src_ref=src, dst_ref=dst, send_sem=ssem.at[which], recv_sem=rsem.at[which],
            device_id=target, device_id_type=LOGICAL,
        )

    def arrived(ref, which):
        send(ref, ref, which, me).wait_recv()

    def sent(ref, which):
        send(ref, ref, which, me).wait_send()

    for load in loads:
        load.wait()
    slots = slot_ref[...]
    owner = slots >> 9
    own_clicks = two_rows(click_ref[pl.ds(2 * feat, 2), :])
    tag = (slots & 511) * 2 + own_clicks + 1
    hot = iota((n_dev, 256), 0) == owner
    hot_half = onehot(hot)
    before = onehot(iota((256, 256), 0) < iota((256, 256), 1))
    counts = dot(hot_half, before)
    rank = jnp.sum(jnp.where(hot, counts, 0.0), axis=0, keepdims=True).astype(i32)
    lane_row = rank + feat * 8
    owner_hot[...] = hot_half
    lane_of[...] = lane_row
    place = owner * 8 + rank
    lane_hot = iota((128, 256), 0) == lane_row

    def by_owner(row):
        return dot_nt(hot_half, jnp.where(lane_hot, row, 0.0).astype(bf16))

    tags = jnp.concatenate(
        [by_owner((tag >> 5).astype(f32)), by_owner((tag & 31).astype(f32))], axis=1
    ).astype(bf16)

    def pack(b, carry):
        base = b * 128
        sel = onehot(iota((128, 256), 0) + base == place)
        extra = onehot(iota((128, 128), 0) + base == iota((128, 128), 1) * 8 + 6)
        out = dot(sel, mfeat_ref[...]) + dot(extra, tags)
        msg[pl.ds(b * 16, 16)] = jnp.concatenate(
            [out[:, :128].reshape(16, 8, 128), out[:, 128:].reshape(16, 8, 128)], axis=1
        ).astype(bf16)
        return carry

    lax.fori_loop(0, 8, pack, 0)

    coef = jnp.broadcast_to(coef_ref[...], (8, coef_ref.shape[1])).astype(bf16)
    for c in range(chunks):
        feature_copy(c).wait()
        out = dot_nt(coef, fbuf[c * rows_chunk : (c + 1) * rows_chunk, :])[0:1]
        for j in range(rows_chunk // 256):
            part[c * (rows_chunk // 256) + j] = out[:, 256 * j : 256 * j + 256]

    pl.semaphore_wait(barrier, n_dev - 1)

    for b in feat_far:
        send(part.at[feats[b]], rs.at[feat], 0, dp * n_feat + feats[b]).start()

    for a, b in all_far[:SPLIT]:
        t = dps[a] * n_feat + feats[b]
        send(msg.at[t], rin.at[me], 1, t).start()

    rs[feat] = part[feat]
    rin[me] = msg[me]

    arrived(rs.at[pl.ds(0, n_feat - 1)], 0)
    score = rs[0]
    for f in range(1, n_feat):
        score = score + rs[f]
    own[...] = score
    ag[feat] = score
    lane_hot = iota((128, 256), 0) == lane_of[...]
    parts = [
        dot_nt(owner_hot[...], jnp.where(lane_hot, t.astype(f32), 0.0).astype(bf16))
        for t in split3(score)
    ]
    by = (parts[0] + parts[1]) + parts[2]
    sc[...] = by.reshape(n_dev, 1, 128)

    for a, b in all_far:
        t = dps[a] * n_feat + feats[b]
        send(sc.at[t], scr.at[me], 2, t).start()

    for a, b in all_far[SPLIT:]:
        t = dps[a] * n_feat + feats[b]
        send(msg.at[t], rin.at[me], 1, t).start()

    for b in feat_far:
        send(own, ag.at[feat], 3, dp * n_feat + feats[b]).start()

    scr[me] = sc[me]

    arrived(rin.at[pl.ds(0, n_dev - 1)], 1)

    def unpack(b, carry):
        got = rin[pl.ds(b * 16, 16)].astype(f32)
        rows_src[pl.ds(b * 128, 128), :] = jnp.concatenate(
            [got[:, 0:8].reshape(128, 128), got[:, 8:16].reshape(128, 128)], axis=1
        ).astype(bf16)
        return carry

    lax.fori_loop(0, 8, unpack, 0)
    src = iota((8, 1024), 1)
    tag_sel = onehot(((src & 7) == 6) & ((src >> 7) == iota((8, 1024), 0)))
    tags_in = dot(tag_sel, rows_src[...])
    tag_in = (tags_in[:, :128] * 32.0 + tags_in[:, 128:]).astype(i32) - 1
    used = tag_in >= 0
    slot_in = jnp.where(used, tag_in >> 1, -1)
    label_in = jnp.where(used, tag_in & 1, 0)

    def line(x):
        return jnp.concatenate([x[a : a + 1] for a in range(8)], axis=1)

    slot_line = line(slot_in)
    member_line = slot_line >> 6
    spot_line = jnp.where(slot_line < 0, -1, slot_line & 63)
    mine = iota((8, 1024), 0) == member_line
    bhot[...] = onehot((iota((128, 1024), 0) & 63) == spot_line)

    for h in range(4):
        sel = onehot(iota((128, 1024), 0) + 128 * h == slot_line)
        padded[128 * h : 128 * h + 128, :] = dot(sel, rows_src[...]).astype(bf16)

    low = iota((32, 128), 1) < 64
    for h in range(4):
        pair = padded[128 * h : 128 * h + 128, :]
        prod = dot_nt(pair, pair)
        turned = pltpu.roll(prod, 64, 1)
        gram[pl.ds(2 * h, 32, stride=8), :] = jnp.where(low, prod[0:32], turned[32:64])
        gram[pl.ds(2 * h + 1, 32, stride=8), :] = jnp.where(low, turned[64:96], prod[96:128])

    marks = jnp.concatenate(
        [jnp.where(mine, line(label_in).astype(f32), 0.0), jnp.where(mine, 1.0, 0.0)], axis=0
    ).astype(bf16)
    marked = dot_nt(marks, bhot[...])
    label, live = marked[0:8], marked[8:16]

    member_of = iota((8, 512), 1) >> 6 == iota((8, 512), 0)
    first = jnp.where(member_of, fold3(dot_nt(stack3(mcoef_ref[...]), padded[...])), 0.0)
    first = (first[:, 0:128] + first[:, 128:256]) + (first[:, 256:384] + first[:, 384:512])
    start = first + pltpu.roll(first, 64, 1)

    arrived(scr.at[pl.ds(0, n_dev - 1)], 2)
    score_in = [jnp.sum(scr[16 * a : 16 * a + 16], axis=0) for a in range(8)]
    score_line = jnp.concatenate(score_in, axis=1)
    offset = fold3(dot_nt(stack3(jnp.where(mine, score_line, 0.0)), bhot[...]))

    lane = iota((8, 128), 1)
    low = lane < 64

    def newton(step, carry):
        u, _ = carry
        prob = jax.nn.sigmoid(offset + u)
        slope = live * (prob - label)
        root = jnp.sqrt(live * prob * (1.0 - prob))
        rhs = root * (gram_times(gram, slope) + u)
        rows = []
        for p in range(32):
            scaled = gram[8 * p : 8 * p + 8, :] * root * take(root, jnp.where(low, p, p + 32))
            diagonal = (lane == p) | (lane == p + 96)
            rows.append(scaled + jnp.where(diagonal, 1.0, 0.0))
        beta = root * solve(rows, rhs) - slope
        return gram_times(gram, beta), beta

    value, beta = lax.fori_loop(0, NEWTON, newton, (start, jnp.zeros((8, 128), f32)))

    back = fold3(dot(stack3(jnp.where(low, value, 0.0)), bhot[...]))
    back = jnp.sum(jnp.where(mine, back, 0.0), axis=0, keepdims=True)
    for a in range(8):
        bk[a] = back[:, 128 * a : 128 * a + 128]

    for a, b in all_far:
        send(bk.at[dps[a]], ret.at[me], 5, dps[a] * n_feat + feats[b]).start()

    ret[me] = bk[dp]

    arrived(ag.at[pl.ds(0, n_feat - 1)], 3)
    scores = jnp.concatenate(
        [ag[f][:, 128 * h : 128 * h + 128] for f in range(n_feat) for h in range(2)], axis=0
    )
    resid = jax.nn.sigmoid(scores + mscore_ref[...]) - click_ref[...].astype(f32)
    grad = jnp.zeros((8, fbuf.shape[1]), f32)
    for b in range(4):
        eight = resid[8 * b : 8 * b + 8]
        wide = jnp.concatenate([eight] * 8, axis=1)
        wide = jnp.where(iota((8, 1024), 1) >> 7 == iota((8, 1024), 0), wide, 0.0).astype(bf16)
        grad = grad + dot(wide, fbuf[1024 * b : 1024 * b + 1024, :])
    gsrc[...] = jnp.sum(grad, axis=0, keepdims=True)

    for a in dp_far:
        send(gsrc, gin.at[dp], 4, dps[a] * n_feat + feat).start()

    gin[dp] = gsrc[...]

    spread = jnp.where(member_of, jnp.concatenate([beta] * 4, axis=1), 0.0)
    out_ref[0:8, :] = fold3(dot(stack3(spread), padded[...]))

    arrived(gin.at[pl.ds(0, n_dp - 1)], 4)
    full = gin[0]
    for t in range(1, n_dp):
        full = full + gin[t]
    full = full / math.sqrt(n_dev * 256)
    out_ref[8:9, :] = full[:, :256]
    out_ref[9:10, :] = full[:, 256:]

    sent(part.at[pl.ds(0, n_feat - 1)], 0)
    sent(msg.at[pl.ds(0, n_dev - 1)], 1)
    sent(sc.at[pl.ds(0, n_dev - 1)], 2)
    sent(ag.at[pl.ds(0, n_feat - 1)], 3)
    sent(gin.at[pl.ds(0, n_dp - 1)], 4)

    arrived(ret.at[pl.ds(0, n_dev - 1)], 5)
    lane_half = onehot(iota((128, 256), 0) == lane_of[...])
    came = ret[...].reshape(n_dev, 128)
    got = [dot(t, lane_half) for t in split3(came)]
    got = (got[0] + got[1]) + got[2]
    mine_back = jnp.sum(jnp.where(iota((n_dev, 256), 0) == slot_ref[...] >> 9, got, 0.0), axis=0)
    out_ref[10:11, :] = own[...] + mine_back[None, :]
    sent(ret.at[pl.ds(0, n_dev - 1)], 5)


def split(merged_ref, grad_ref, coefs_ref, total_ref):
    coefs_ref[...] = merged_ref[0:8, :]
    grad_ref[...] = jnp.concatenate([merged_ref[8:9, :], merged_ref[9:10, :]], axis=1)
    total_ref[...] = merged_ref[10:11, :]


def per_device(
    features, fixed_coef, member_score, clicks, member_features, member_coef, block_slot
):
    n_dev = 128
    rows, width = features.shape
    vmem = pl.BlockSpec(memory_space=pltpu.VMEM)
    merged = pl.pallas_call(
        kernel,
        name="glmix",
        out_shape=pltpu.VMEM((16, 256), f32),
        in_specs=[pl.BlockSpec(memory_space=pltpu.HBM)] * 7,
        out_specs=vmem,
        scratch_shapes=[
            pltpu.VMEM((1, width), f32),
            pltpu.VMEM((rows // 128, 128), f32),
            pltpu.VMEM((rows // 128, 128), i32),
            pltpu.VMEM(member_features.shape, bf16),
            pltpu.VMEM(member_coef.shape, f32),
            pltpu.VMEM((1, 256), i32),
            pltpu.VMEM((rows, width), bf16),
            pltpu.VMEM((n_dev, 16, 128), bf16),
            pltpu.VMEM((n_dev, 16, 128), bf16),
            pltpu.VMEM((16, 1, 256), f32),
            pltpu.VMEM((16, 1, 256), f32),
            pltpu.VMEM((1, 256), f32),
            pltpu.VMEM((16, 1, 256), f32),
            pltpu.VMEM((n_dev, 1, 128), f32),
            pltpu.VMEM((n_dev, 1, 128), f32),
            pltpu.VMEM((8, 1, 128), f32),
            pltpu.VMEM((n_dev, 1, 128), f32),
            pltpu.VMEM((1, width), f32),
            pltpu.VMEM((8, 1, width), f32),
            pltpu.VMEM((n_dev, 256), bf16),
            pltpu.VMEM((1, 256), i32),
            pltpu.VMEM((1024, 256), bf16),
            pltpu.VMEM((128, 1024), bf16),
            pltpu.VMEM((512, 256), bf16),
            pltpu.VMEM((256, 128), f32),
            pltpu.SemaphoreType.DMA((6,)),
            pltpu.SemaphoreType.DMA((8,)),
            pltpu.SemaphoreType.DMA((6,)),
            pltpu.SemaphoreType.DMA((6,)),
        ],
        compiler_params=pltpu.CompilerParams(collective_id=0, has_side_effects=True),
    )(
        fixed_coef.reshape(1, width),
        member_score.reshape(rows // 128, 128),
        clicks.reshape(rows // 128, 128),
        member_features,
        member_coef,
        block_slot.reshape(1, -1),
        features,
    )
    grad, coefs, total = pl.pallas_call(
        split,
        name="split",
        out_shape=(
            jax.ShapeDtypeStruct((1, width), f32),
            jax.ShapeDtypeStruct(member_coef.shape, f32),
            jax.ShapeDtypeStruct((1, block_slot.shape[0]), f32),
        ),
        in_specs=[vmem],
        out_specs=(vmem,) * 3,
        compiler_params=pltpu.CompilerParams(vmem_limit_bytes=1 << 20),
    )(merged)
    return grad.reshape(-1), coefs, total.reshape(-1)


def solution(mesh):
    return jax.shard_map(
        per_device,
        mesh=mesh,
        in_specs=(
            P("dp", "feat"),
            P("feat"),
            P("dp"),
            P("dp"),
            P(("dp", "feat"), None),
            P(("dp", "feat"), None),
            P(("dp", "feat")),
        ),
        out_specs=(P("feat"), P(("dp", "feat"), None), P(("dp", "feat"))),
        check_vma=False,
    )
```

```python
import math

import jax
import jax.numpy as jnp
from jax import lax
from jax.experimental import pallas as pl
from jax.experimental.pallas import tpu as pltpu
from jax.sharding import PartitionSpec as P

SPLIT = 104
LOGICAL = pl.DeviceIdType.LOGICAL
BLK = 64
NEWTON = 3
GROUPS = 2
f32, bf16, i32 = jnp.float32, jnp.bfloat16, jnp.int32


def iota(shape, dim):
    return lax.broadcasted_iota(i32, shape, dim)


def dot(a, b):
    return lax.dot_general(a, b, (((1,), (0,)), ((), ())), preferred_element_type=f32)


def dot_nt(a, b):
    return lax.dot_general(a, b, (((1,), (1,)), ((), ())), preferred_element_type=f32)


def split3(x):
    high = x.astype(bf16)
    rest = x - high.astype(f32)
    mid = rest.astype(bf16)
    low = (rest - mid.astype(f32)).astype(bf16)
    return high, mid, low


def stack3(x):
    return jnp.concatenate([t.astype(f32) for t in split3(x)], axis=0).astype(bf16)


def fold3(y):
    n = y.shape[0] // 3
    return (y[:n] + y[n : 2 * n]) + y[2 * n :]


def onehot(mask):
    return jnp.where(mask, 1.0, 0.0).astype(bf16)


def two_rows(x):
    return jnp.concatenate([x[0:1], x[1:2]], axis=1)


def take(x, index):
    return jnp.take_along_axis(x, index, axis=1, mode="promise_in_bounds")


def solve(rows, y):
    lane = iota((8, 128), 1)
    side = lane & 31
    base = lane - side
    group = lane & 15
    rows = [list(pair) for pair in rows]
    s = [jnp.zeros((8, 128), f32)] * 2
    for q in range(0, 16, GROUPS):
        unknowns = [16 * r + g for r in range(4) for g in range(q, q + GROUPS)]
        n = len(unknowns)

        def at(x, place):
            return jnp.broadcast_to(x[:, place : place + 1], (8, 128))

        block = {}
        for j, v in enumerate(unknowns):
            for i, w in enumerate(unknowns[: j + 1]):
                block[i, j] = at(rows[w % 16][v // 32], 32 * (w // 16) + v % 32)
        ys = [at(y[v // 32], v % 32) for v in unknowns]
        inside = (group >= q) & (group < q + GROUPS)
        done = group < q + GROUPS
        t = []
        for v in unknowns:
            own = [take(rows[v % 16][h], side + 32 * (v // 16)) for h in range(2)]
            own = [jnp.where(inside, 0.0, x) for x in own]
            own[v // 32] = jnp.where(side == v % 32, 1.0, own[v // 32])
            t.append(own)
        invs, factor = {}, {}
        for k in range(0, n, 2):
            a, b, c = block[k, k], block[k, k + 1], block[k + 1, k + 1]
            scale = 1.0 / (a * c - b * b)
            invs[k] = (c * scale, b * scale, a * scale)
            for i in range(k + 2, n):
                factor[i, k] = (c * block[k, i] - b * block[k + 1, i]) * scale
                factor[i, k + 1] = (a * block[k + 1, i] - b * block[k, i]) * scale
            for i in range(k + 2, n):
                for j in range(i, n):
                    block[i, j] = block[i, j] - (
                        factor[i, k] * block[k, j] + factor[i, k + 1] * block[k + 1, j]
                    )
                for h in range(2):
                    t[i][h] = t[i][h] - (
                        factor[i, k] * t[k][h] + factor[i, k + 1] * t[k + 1][h]
                    )
        for k in range(0, n, 2):
            a, b, c = invs[k]
            for h in range(2):
                t[k][h], t[k + 1][h] = (
                    a * t[k][h] - b * t[k + 1][h],
                    c * t[k + 1][h] - b * t[k][h],
                )
        for k in range(n - 2, 0, -2):
            for i in range(k):
                for h in range(2):
                    t[i][h] = t[i][h] - (factor[k, i] * t[k][h] + factor[k + 1, i] * t[k + 1][h])
        step = [tree_sum([ys[i] * t[i][h] for i in range(n)]) for h in range(2)]
        s = [s[h] + jnp.where(done, step[h], 0.0) for h in range(2)]
        y = [y[h] - jnp.where(done, 0.0, step[h]) for h in range(2)]
        for part in (range(q + GROUPS, min(q + 2 * GROUPS, 16)), range(q + 2 * GROUPS, 16)):
            picks = [
                [take(rows[g][v // 32], base + v % 32) for g in part] for v in unknowns
            ]
            for at_, g in enumerate(part):
                for h in range(2):
                    change = tree_sum([picks[i][at_] * t[i][h] for i in range(n)])
                    rows[g][h] = jnp.where(inside, 0.0, rows[g][h]) - change
    return s


def tree_sum(terms):
    while len(terms) > 1:
        terms = [sum(terms[i + 1 : i + 2], terms[i]) for i in range(0, len(terms), 2)]
    return terms[0]


def by_rows(v, g):
    lane = iota((8, 128), 1)
    r = lane >> 5
    return take(jnp.where(lane < 64, v[0], v[1]), 32 * r + 16 * (r & 1) + g)


def gram_times(gram_ref, v):
    picks = [by_rows(v, g) for g in range(16)]
    out = []
    for h in range(2):
        total = tree_sum(
            [gram_ref[16 * g + 8 * h : 16 * g + 8 * h + 8, :] * picks[g] for g in range(16)]
        )
        turns = [pltpu.roll(total, shift, 1) for shift in (32, 64, 96)]
        out.append((total + turns[0]) + (turns[1] + turns[2]))
    return out


def kernel(
    coef_hbm, mscore_hbm, click_hbm, mfeat_hbm, mcoef_hbm, slot_hbm, feat_ref,
    out_ref,
    coef_ref, mscore_ref, click_ref, mfeat_ref, mcoef_ref, slot_ref,
    fbuf, msg, rin, part, rs, own, ag, sc, scr, bk, ret, gsrc, gin,
    owner_hot, lane_of, rows_src, bhot, padded, gram,
    isem, fsem, ssem, rsem,
):
    n_dp, n_feat = 8, 16
    n_dev = n_dp * n_feat
    dp, feat = lax.axis_index("dp"), lax.axis_index("feat")
    me = dp * n_feat + feat

    chunks = 8
    rows_chunk = fbuf.shape[0] // chunks

    def feature_copy(c):
        window = pl.ds(c * rows_chunk, rows_chunk)
        return pltpu.make_async_copy(feat_ref.at[window], fbuf.at[window], fsem.at[c])

    loads = [
        pltpu.make_async_copy(src, dst, isem.at[i])
        for i, (src, dst) in enumerate([
            (slot_hbm, slot_ref), (click_hbm, click_ref), (mfeat_hbm, mfeat_ref),
            (coef_hbm, coef_ref), (mscore_hbm, mscore_ref), (mcoef_hbm, mcoef_ref),
        ])
    ]
    for load in loads:
        load.start()
    for c in range(chunks):
        feature_copy(c).start()

    barrier = pltpu.get_barrier_semaphore()

    dps = [2 * lax.rem(dp // 2 + dy, 4) + lax.rem(dp + dc, 2) for dy in range(4) for dc in range(2)]
    feats = [
        4 * lax.rem(feat // 4 + dz, 4) + lax.rem(feat + dx, 4) for dz in range(4) for dx in range(4)
    ]
    hops = [0, 1, 2, 1]
    dp_far = sorted(range(1, 8), key=lambda a: -hops[a // 2])
    feat_far = sorted(range(1, 16), key=lambda b: -hops[b // 4] - hops[b % 4])
    all_far = sorted(
        ((a, b) for a in range(8) for b in range(16) if a or b),
        key=lambda ab: -hops[ab[0] // 2] - hops[ab[1] // 4] - hops[ab[1] % 4],
    )

    for a, b in all_far:
        pl.semaphore_signal(
            barrier, inc=1, device_id=dps[a] * n_feat + feats[b], device_id_type=LOGICAL
        )

    def send(src, dst, which, target):
        return pltpu.make_async_remote_copy(
            src_ref=src, dst_ref=dst, send_sem=ssem.at[which], recv_sem=rsem.at[which],
            device_id=target, device_id_type=LOGICAL,
        )

    def arrived(ref, which):
        send(ref, ref, which, me).wait_recv()

    def sent(ref, which):
        send(ref, ref, which, me).wait_send()

    for load in loads:
        load.wait()
    slots = slot_ref[...]
    owner = slots >> 9
    own_clicks = two_rows(click_ref[pl.ds(2 * feat, 2), :])
    tag = (slots & 511) * 2 + own_clicks + 1
    hot = iota((n_dev, 256), 0) == owner
    hot_half = onehot(hot)
    before = onehot(iota((256, 256), 0) < iota((256, 256), 1))
    counts = dot(hot_half, before)
    rank = jnp.sum(jnp.where(hot, counts, 0.0), axis=0, keepdims=True).astype(i32)
    lane_row = rank + feat * 8
    owner_hot[...] = hot_half
    lane_of[...] = lane_row
    place = owner * 8 + rank
    lane_hot = iota((128, 256), 0) == lane_row

    def by_owner(row):
        return dot_nt(hot_half, jnp.where(lane_hot, row, 0.0).astype(bf16))

    tags = jnp.concatenate(
        [by_owner((tag >> 5).astype(f32)), by_owner((tag & 31).astype(f32))], axis=1
    ).astype(bf16)

    def pack(b, carry):
        base = b * 128
        sel = onehot(iota((128, 256), 0) + base == place)
        extra = onehot(iota((128, 128), 0) + base == iota((128, 128), 1) * 8 + 6)
        out = dot(sel, mfeat_ref[...]) + dot(extra, tags)
        msg[pl.ds(b * 16, 16)] = jnp.concatenate(
            [out[:, :128].reshape(16, 8, 128), out[:, 128:].reshape(16, 8, 128)], axis=1
        ).astype(bf16)
        return carry

    for b in range(8):
        pack(b, 0)

    coef = jnp.broadcast_to(coef_ref[...], (8, coef_ref.shape[1])).astype(bf16)
    for c in range(chunks):
        feature_copy(c).wait()
        out = dot_nt(coef, fbuf[c * rows_chunk : (c + 1) * rows_chunk, :])[0:1]
        for j in range(rows_chunk // 256):
            part[c * (rows_chunk // 256) + j] = out[:, 256 * j : 256 * j + 256]

    pl.semaphore_wait(barrier, n_dev - 1)

    for b in feat_far:
        send(part.at[feats[b]], rs.at[feat], 0, dp * n_feat + feats[b]).start()

    for a, b in all_far[:SPLIT]:
        t = dps[a] * n_feat + feats[b]
        send(msg.at[t], rin.at[me], 1, t).start()

    rs[feat] = part[feat]
    rin[me] = msg[me]

    arrived(rs.at[pl.ds(0, n_feat - 1)], 0)
    score = rs[0]
    for f in range(1, n_feat):
        score = score + rs[f]
    own[...] = score
    ag[feat] = score
    lane_hot = iota((128, 256), 0) == lane_of[...]
    parts = [
        dot_nt(owner_hot[...], jnp.where(lane_hot, t.astype(f32), 0.0).astype(bf16))
        for t in split3(score)
    ]
    by = (parts[0] + parts[1]) + parts[2]
    sc[...] = by.reshape(n_dev, 1, 128)

    for a, b in all_far:
        t = dps[a] * n_feat + feats[b]
        send(sc.at[t], scr.at[me], 2, t).start()

    for a, b in all_far[SPLIT:]:
        t = dps[a] * n_feat + feats[b]
        send(msg.at[t], rin.at[me], 1, t).start()

    for b in feat_far:
        send(own, ag.at[feat], 3, dp * n_feat + feats[b]).start()

    scr[me] = sc[me]

    arrived(rin.at[pl.ds(0, n_dev - 1)], 1)

    def unpack(b, carry):
        got = rin[pl.ds(b * 16, 16)].astype(f32)
        rows_src[pl.ds(b * 128, 128), :] = jnp.concatenate(
            [got[:, 0:8].reshape(128, 128), got[:, 8:16].reshape(128, 128)], axis=1
        ).astype(bf16)
        return carry

    lax.fori_loop(0, 8, unpack, 0)
    src = iota((8, 1024), 1)
    tag_sel = onehot(((src & 7) == 6) & ((src >> 7) == iota((8, 1024), 0)))
    tags_in = dot(tag_sel, rows_src[...])
    tag_in = (tags_in[:, :128] * 32.0 + tags_in[:, 128:]).astype(i32) - 1
    used = tag_in >= 0
    slot_in = jnp.where(used, tag_in >> 1, -1)
    label_in = jnp.where(used, tag_in & 1, 0)

    def line(x):
        return jnp.concatenate([x[a : a + 1] for a in range(8)], axis=1)

    slot_line = line(slot_in)
    member_line = slot_line >> 6
    spot_line = jnp.where(slot_line < 0, -1, slot_line & 63)
    mine = iota((8, 1024), 0) == member_line
    bhot[...] = onehot((iota((128, 1024), 0) & 63) == spot_line)

    for h in range(4):
        sel = onehot(iota((128, 1024), 0) + 128 * h == slot_line)
        padded[128 * h : 128 * h + 128, :] = dot(sel, rows_src[...]).astype(bf16)

    quarter = iota((16, 128), 1) >> 5
    for m in range(8):
        first = 64 * (m % 2)
        if first == 0:
            pair = padded[64 * m : 64 * m + 128, :]
            prod = dot_nt(pair, pair)
        for h in range(2):
            piece = None
            for r in range(4):
                shift = (32 * r - first - 32 * h) % 128
                lines = prod[first + 16 * r : first + 16 * r + 16]
                lines = pltpu.roll(lines, shift, 1) if shift else lines
                piece = lines if piece is None else jnp.where(quarter == r, lines, piece)
            gram[pl.ds(8 * h + m, 16, stride=16), :] = piece

    marks = jnp.concatenate(
        [jnp.where(mine, line(label_in).astype(f32), 0.0), jnp.where(mine, 1.0, 0.0)], axis=0
    ).astype(bf16)
    marked = dot_nt(marks, bhot[...])
    label, live = marked[0:8], marked[8:16]

    member_of = iota((8, 512), 1) >> 6 == iota((8, 512), 0)
    first = jnp.where(member_of, fold3(dot_nt(stack3(mcoef_ref[...]), padded[...])), 0.0)
    first = (first[:, 0:128] + first[:, 128:256]) + (first[:, 256:384] + first[:, 384:512])
    start = first + pltpu.roll(first, 64, 1)

    arrived(scr.at[pl.ds(0, n_dev - 1)], 2)
    score_in = [jnp.sum(scr[16 * a : 16 * a + 16], axis=0) for a in range(8)]
    score_line = jnp.concatenate(score_in, axis=1)
    offset = fold3(dot_nt(stack3(jnp.where(mine, score_line, 0.0)), bhot[...]))

    lane = iota((8, 128), 1)

    def halves(x):
        return [take(x, (lane & 31) + 32 * h) for h in range(2)]

    def joined(v):
        return jnp.where((lane >> 5) & 1 == 0, v[0], v[1])

    offset, live, label, start = halves(offset), halves(live), halves(label), halves(start)

    def newton(step, carry):
        u = carry[0:2]
        prob = [jax.nn.sigmoid(offset[h] + u[h]) for h in range(2)]
        slope = [live[h] * (prob[h] - label[h]) for h in range(2)]
        root = [jnp.sqrt(live[h] * prob[h] * (1.0 - prob[h])) for h in range(2)]
        pull = gram_times(gram, slope)
        rows = []
        for g in range(16):
            across = by_rows(root, g)
            pair = []
            for h in range(2):
                scaled = gram[16 * g + 8 * h : 16 * g + 8 * h + 8, :] * root[h] * across
                diagonal = 16 * (lane >> 5) + g == 32 * h + (lane & 31)
                pair.append(scaled + jnp.where(diagonal, 1.0, 0.0))
            rows.append(pair)
        solved = solve(rows, [root[h] * (pull[h] + u[h]) for h in range(2)])
        beta = [root[h] * solved[h] - slope[h] for h in range(2)]
        return tuple(gram_times(gram, beta)) + tuple(beta)

    zero = jnp.zeros((8, 128), f32)
    final = lax.fori_loop(0, NEWTON, newton, tuple(start) + (zero, zero))
    value, beta = joined(final[0:2]), joined(final[2:4])

    back = fold3(dot(stack3(jnp.where(lane < 64, value, 0.0)), bhot[...]))
    back = jnp.sum(jnp.where(mine, back, 0.0), axis=0, keepdims=True)
    for a in range(8):
        bk[a] = back[:, 128 * a : 128 * a + 128]

    for a, b in all_far:
        send(bk.at[dps[a]], ret.at[me], 5, dps[a] * n_feat + feats[b]).start()

    ret[me] = bk[dp]

    arrived(ag.at[pl.ds(0, n_feat - 1)], 3)
    scores = jnp.concatenate(
        [ag[f][:, 128 * h : 128 * h + 128] for f in range(n_feat) for h in range(2)], axis=0
    )
    resid = jax.nn.sigmoid(scores + mscore_ref[...]) - click_ref[...].astype(f32)
    grad = jnp.zeros((8, fbuf.shape[1]), f32)
    for b in range(4):
        eight = resid[8 * b : 8 * b + 8]
        wide = jnp.concatenate([eight] * 8, axis=1)
        wide = jnp.where(iota((8, 1024), 1) >> 7 == iota((8, 1024), 0), wide, 0.0).astype(bf16)
        grad = grad + dot(wide, fbuf[1024 * b : 1024 * b + 1024, :])
    gsrc[...] = jnp.sum(grad, axis=0, keepdims=True)

    for a in dp_far:
        send(gsrc, gin.at[dp], 4, dps[a] * n_feat + feat).start()

    gin[dp] = gsrc[...]

    spread = jnp.where(member_of, jnp.concatenate([beta] * 4, axis=1), 0.0)
    out_ref[0:8, :] = fold3(dot(stack3(spread), padded[...]))

    arrived(gin.at[pl.ds(0, n_dp - 1)], 4)
    full = gin[0]
    for t in range(1, n_dp):
        full = full + gin[t]
    full = full / math.sqrt(n_dev * 256)
    out_ref[8:9, :] = full[:, :256]
    out_ref[9:10, :] = full[:, 256:]

    sent(part.at[pl.ds(0, n_feat - 1)], 0)
    sent(msg.at[pl.ds(0, n_dev - 1)], 1)
    sent(sc.at[pl.ds(0, n_dev - 1)], 2)
    sent(ag.at[pl.ds(0, n_feat - 1)], 3)
    sent(gin.at[pl.ds(0, n_dp - 1)], 4)

    arrived(ret.at[pl.ds(0, n_dev - 1)], 5)
    lane_half = onehot(iota((128, 256), 0) == lane_of[...])
    came = ret[...].reshape(n_dev, 128)
    got = [dot(t, lane_half) for t in split3(came)]
    got = (got[0] + got[1]) + got[2]
    mine_back = jnp.sum(jnp.where(iota((n_dev, 256), 0) == slot_ref[...] >> 9, got, 0.0), axis=0)
    out_ref[10:11, :] = own[...] + mine_back[None, :]
    sent(ret.at[pl.ds(0, n_dev - 1)], 5)


def split(merged_ref, grad_ref, coefs_ref, total_ref):
    coefs_ref[...] = merged_ref[0:8, :]
    grad_ref[...] = jnp.concatenate([merged_ref[8:9, :], merged_ref[9:10, :]], axis=1)
    total_ref[...] = merged_ref[10:11, :]


def per_device(
    features, fixed_coef, member_score, clicks, member_features, member_coef, block_slot
):
    n_dev = 128
    rows, width = features.shape
    vmem = pl.BlockSpec(memory_space=pltpu.VMEM)
    merged = pl.pallas_call(
        kernel,
        name="glmix",
        out_shape=pltpu.VMEM((16, 256), f32),
        in_specs=[pl.BlockSpec(memory_space=pltpu.HBM)] * 7,
        out_specs=vmem,
        scratch_shapes=[
            pltpu.VMEM((1, width), f32),
            pltpu.VMEM((rows // 128, 128), f32),
            pltpu.VMEM((rows // 128, 128), i32),
            pltpu.VMEM(member_features.shape, bf16),
            pltpu.VMEM(member_coef.shape, f32),
            pltpu.VMEM((1, 256), i32),
            pltpu.VMEM((rows, width), bf16),
            pltpu.VMEM((n_dev, 16, 128), bf16),
            pltpu.VMEM((n_dev, 16, 128), bf16),
            pltpu.VMEM((16, 1, 256), f32),
            pltpu.VMEM((16, 1, 256), f32),
            pltpu.VMEM((1, 256), f32),
            pltpu.VMEM((16, 1, 256), f32),
            pltpu.VMEM((n_dev, 1, 128), f32),
            pltpu.VMEM((n_dev, 1, 128), f32),
            pltpu.VMEM((8, 1, 128), f32),
            pltpu.VMEM((n_dev, 1, 128), f32),
            pltpu.VMEM((1, width), f32),
            pltpu.VMEM((8, 1, width), f32),
            pltpu.VMEM((n_dev, 256), bf16),
            pltpu.VMEM((1, 256), i32),
            pltpu.VMEM((1024, 256), bf16),
            pltpu.VMEM((128, 1024), bf16),
            pltpu.VMEM((512, 256), bf16),
            pltpu.VMEM((256, 128), f32),
            pltpu.SemaphoreType.DMA((6,)),
            pltpu.SemaphoreType.DMA((8,)),
            pltpu.SemaphoreType.DMA((6,)),
            pltpu.SemaphoreType.DMA((6,)),
        ],
        compiler_params=pltpu.CompilerParams(collective_id=0, has_side_effects=True),
    )(
        fixed_coef.reshape(1, width),
        member_score.reshape(rows // 128, 128),
        clicks.reshape(rows // 128, 128),
        member_features,
        member_coef,
        block_slot.reshape(1, -1),
        features,
    )
    grad, coefs, total = pl.pallas_call(
        split,
        name="split",
        out_shape=(
            jax.ShapeDtypeStruct((1, width), f32),
            jax.ShapeDtypeStruct(member_coef.shape, f32),
            jax.ShapeDtypeStruct((1, block_slot.shape[0]), f32),
        ),
        in_specs=[vmem],
        out_specs=(vmem,) * 3,
        compiler_params=pltpu.CompilerParams(vmem_limit_bytes=1 << 20),
    )(merged)
    return grad.reshape(-1), coefs, total.reshape(-1)


def solution(mesh):
    return jax.shard_map(
        per_device,
        mesh=mesh,
        in_specs=(
            P("dp", "feat"),
            P("feat"),
            P("dp"),
            P("dp"),
            P(("dp", "feat"), None),
            P(("dp", "feat"), None),
            P(("dp", "feat")),
        ),
        out_specs=(P("feat"), P(("dp", "feat"), None), P(("dp", "feat"))),
        check_vma=False,
    )
```

```python
import math

import jax
import jax.numpy as jnp
from jax import lax
from jax.experimental import pallas as pl
from jax.experimental.pallas import tpu as pltpu
from jax.sharding import PartitionSpec as P

SPLIT = 84
LOGICAL = pl.DeviceIdType.LOGICAL
BLK = 64
NEWTON = 3
GROUPS = 2
f32, bf16, i32 = jnp.float32, jnp.bfloat16, jnp.int32


def iota(shape, dim):
    return lax.broadcasted_iota(i32, shape, dim)


def dot(a, b):
    return lax.dot_general(a, b, (((1,), (0,)), ((), ())), preferred_element_type=f32)


def dot_nt(a, b):
    return lax.dot_general(a, b, (((1,), (1,)), ((), ())), preferred_element_type=f32)


def split3(x):
    high = x.astype(bf16)
    rest = x - high.astype(f32)
    mid = rest.astype(bf16)
    low = (rest - mid.astype(f32)).astype(bf16)
    return high, mid, low


def stack3(x):
    return jnp.concatenate([t.astype(f32) for t in split3(x)], axis=0).astype(bf16)


def fold3(y):
    n = y.shape[0] // 3
    return (y[:n] + y[n : 2 * n]) + y[2 * n :]


def onehot(mask):
    return jnp.where(mask, 1.0, 0.0).astype(bf16)


def two_rows(x):
    return jnp.concatenate([x[0:1], x[1:2]], axis=1)


def take(x, index):
    return jnp.take_along_axis(x, index, axis=1, mode="promise_in_bounds")


def solve(rows, y):
    lane = iota((8, 128), 1)
    side = lane & 31
    base = lane - side
    group = lane & 15
    rows = [list(pair) for pair in rows]
    s = [jnp.zeros((8, 128), f32)] * 2
    for q in range(0, 16, GROUPS):
        unknowns = [16 * r + g for r in range(4) for g in range(q, q + GROUPS)]
        n = len(unknowns)

        def at(x, place):
            return jnp.broadcast_to(x[:, place : place + 1], (8, 128))

        block = {}
        for j, v in enumerate(unknowns):
            for i, w in enumerate(unknowns[: j + 1]):
                block[i, j] = at(rows[w % 16][v // 32], 32 * (w // 16) + v % 32)
        ys = [at(y[v // 32], v % 32) for v in unknowns]
        inside = (group >= q) & (group < q + GROUPS)
        done = group < q + GROUPS
        t = []
        for v in unknowns:
            own = [take(rows[v % 16][h], side + 32 * (v // 16)) for h in range(2)]
            own = [jnp.where(inside, 0.0, x) for x in own]
            own[v // 32] = jnp.where(side == v % 32, 1.0, own[v // 32])
            t.append(own)
        invs, factor = {}, {}
        for k in range(0, n, 2):
            a, b, c = block[k, k], block[k, k + 1], block[k + 1, k + 1]
            scale = 1.0 / (a * c - b * b)
            invs[k] = (c * scale, b * scale, a * scale)
            for i in range(k + 2, n):
                factor[i, k] = (c * block[k, i] - b * block[k + 1, i]) * scale
                factor[i, k + 1] = (a * block[k + 1, i] - b * block[k, i]) * scale
            for i in range(k + 2, n):
                for j in range(i, n):
                    block[i, j] = block[i, j] - (
                        factor[i, k] * block[k, j] + factor[i, k + 1] * block[k + 1, j]
                    )
                for h in range(2):
                    t[i][h] = t[i][h] - (
                        factor[i, k] * t[k][h] + factor[i, k + 1] * t[k + 1][h]
                    )
        for k in range(0, n, 2):
            a, b, c = invs[k]
            for h in range(2):
                t[k][h], t[k + 1][h] = (
                    a * t[k][h] - b * t[k + 1][h],
                    c * t[k + 1][h] - b * t[k][h],
                )
        for k in range(n - 2, 0, -2):
            for i in range(k):
                for h in range(2):
                    t[i][h] = t[i][h] - (factor[k, i] * t[k][h] + factor[k + 1, i] * t[k + 1][h])
        step = [tree_sum([ys[i] * t[i][h] for i in range(n)]) for h in range(2)]
        s = [s[h] + jnp.where(done, step[h], 0.0) for h in range(2)]
        y = [y[h] - jnp.where(done, 0.0, step[h]) for h in range(2)]
        for part in (range(q + GROUPS, min(q + 2 * GROUPS, 16)), range(q + 2 * GROUPS, 16)):
            picks = [
                [take(rows[g][v // 32], base + v % 32) for g in part] for v in unknowns
            ]
            for at_, g in enumerate(part):
                for h in range(2):
                    change = tree_sum([picks[i][at_] * t[i][h] for i in range(n)])
                    rows[g][h] = jnp.where(inside, 0.0, rows[g][h]) - change
    return s


def tree_sum(terms):
    while len(terms) > 1:
        terms = [sum(terms[i + 1 : i + 2], terms[i]) for i in range(0, len(terms), 2)]
    return terms[0]


def by_rows(v, g):
    lane = iota((8, 128), 1)
    r = lane >> 5
    return take(jnp.where(lane < 64, v[0], v[1]), 32 * r + 16 * (r & 1) + g)


def gram_times(gram_ref, v):
    picks = [by_rows(v, g) for g in range(16)]
    out = []
    for h in range(2):
        total = tree_sum(
            [gram_ref[16 * g + 8 * h : 16 * g + 8 * h + 8, :] * picks[g] for g in range(16)]
        )
        turns = [pltpu.roll(total, shift, 1) for shift in (32, 64, 96)]
        out.append((total + turns[0]) + (turns[1] + turns[2]))
    return out


def kernel(
    coef_hbm, mscore_hbm, click_hbm, mfeat_hbm, mcoef_hbm, slot_hbm, feat_ref,
    out_ref,
    coef_ref, mscore_ref, click_ref, mfeat_ref, mcoef_ref, slot_ref,
    fbuf, msg, rin, part, rs, own, ag, sc, scr, bk, ret, gsrc, gin,
    owner_hot, lane_of, rows_src, bhot, padded, gram,
    isem, fsem, ssem, rsem,
):
    n_dp, n_feat = 8, 16
    n_dev = n_dp * n_feat
    dp, feat = lax.axis_index("dp"), lax.axis_index("feat")
    me = dp * n_feat + feat

    chunks = 8
    rows_chunk = fbuf.shape[0] // chunks

    def feature_copy(c):
        window = pl.ds(c * rows_chunk, rows_chunk)
        return pltpu.make_async_copy(feat_ref.at[window], fbuf.at[window], fsem.at[c])

    loads = [
        pltpu.make_async_copy(src, dst, isem.at[i])
        for i, (src, dst) in enumerate([
            (slot_hbm, slot_ref), (click_hbm, click_ref), (mfeat_hbm, mfeat_ref),
            (coef_hbm, coef_ref), (mscore_hbm, mscore_ref), (mcoef_hbm, mcoef_ref),
        ])
    ]
    for load in loads:
        load.start()
    for c in range(chunks):
        feature_copy(c).start()

    barrier = pltpu.get_barrier_semaphore()

    dps = [2 * lax.rem(dp // 2 + dy, 4) + lax.rem(dp + dc, 2) for dy in range(4) for dc in range(2)]
    feats = [
        4 * lax.rem(feat // 4 + dz, 4) + lax.rem(feat + dx, 4) for dz in range(4) for dx in range(4)
    ]
    hops = [0, 1, 2, 1]
    dp_far = sorted(range(1, 8), key=lambda a: -hops[a // 2])
    feat_far = sorted(range(1, 16), key=lambda b: -hops[b // 4] - hops[b % 4])
    all_far = sorted(
        ((a, b) for a in range(8) for b in range(16) if a or b),
        key=lambda ab: -hops[ab[0] // 2] - hops[ab[1] // 4] - hops[ab[1] % 4],
    )

    for a, b in all_far:
        pl.semaphore_signal(
            barrier, inc=1, device_id=dps[a] * n_feat + feats[b], device_id_type=LOGICAL
        )

    def send(src, dst, which, target):
        return pltpu.make_async_remote_copy(
            src_ref=src, dst_ref=dst, send_sem=ssem.at[which], recv_sem=rsem.at[which],
            device_id=target, device_id_type=LOGICAL,
        )

    def arrived(ref, which):
        send(ref, ref, which, me).wait_recv()

    def sent(ref, which):
        send(ref, ref, which, me).wait_send()

    for load in loads:
        load.wait()
    slots = slot_ref[...]
    owner = slots >> 9
    own_clicks = two_rows(click_ref[pl.ds(2 * feat, 2), :])
    tag = (slots & 511) * 2 + own_clicks + 1
    hot = iota((n_dev, 256), 0) == owner
    hot_half = onehot(hot)
    before = onehot(iota((256, 256), 0) < iota((256, 256), 1))
    counts = dot(hot_half, before)
    rank = jnp.sum(jnp.where(hot, counts, 0.0), axis=0, keepdims=True).astype(i32)
    lane_row = rank + feat * 8
    owner_hot[...] = hot_half
    lane_of[...] = lane_row
    place = owner * 8 + rank
    lane_hot = iota((128, 256), 0) == lane_row

    def by_owner(row):
        return dot_nt(hot_half, jnp.where(lane_hot, row, 0.0).astype(bf16))

    tags = jnp.concatenate(
        [by_owner((tag >> 5).astype(f32)), by_owner((tag & 31).astype(f32))], axis=1
    ).astype(bf16)

    def pack(b, carry):
        base = b * 128
        sel = onehot(iota((128, 256), 0) + base == place)
        extra = onehot(iota((128, 128), 0) + base == iota((128, 128), 1) * 8 + 6)
        out = dot(sel, mfeat_ref[...]) + dot(extra, tags)
        msg[pl.ds(b * 16, 16)] = jnp.concatenate(
            [out[:, :128].reshape(16, 8, 128), out[:, 128:].reshape(16, 8, 128)], axis=1
        ).astype(bf16)
        return carry

    for b in range(8):
        pack(b, 0)

    coef = jnp.broadcast_to(coef_ref[...], (8, coef_ref.shape[1])).astype(bf16)
    for c in range(chunks):
        feature_copy(c).wait()
        out = dot_nt(coef, fbuf[c * rows_chunk : (c + 1) * rows_chunk, :])[0:1]
        for j in range(rows_chunk // 256):
            part[c * (rows_chunk // 256) + j] = out[:, 256 * j : 256 * j + 256]

    pl.semaphore_wait(barrier, n_dev - 1)

    for b in feat_far:
        send(part.at[feats[b]], rs.at[feat], 0, dp * n_feat + feats[b]).start()

    for a, b in all_far[:SPLIT]:
        t = dps[a] * n_feat + feats[b]
        send(msg.at[t], rin.at[me], 1, t).start()

    rs[feat] = part[feat]
    rin[me] = msg[me]

    arrived(rs.at[pl.ds(0, n_feat - 1)], 0)
    score = rs[0]
    for f in range(1, n_feat):
        score = score + rs[f]
    own[...] = score
    ag[feat] = score
    lane_hot = iota((128, 256), 0) == lane_of[...]
    parts = [
        dot_nt(owner_hot[...], jnp.where(lane_hot, t.astype(f32), 0.0).astype(bf16))
        for t in split3(score)
    ]
    by = (parts[0] + parts[1]) + parts[2]
    sc[...] = by.reshape(n_dev, 1, 128)

    for a, b in all_far:
        t = dps[a] * n_feat + feats[b]
        send(sc.at[t], scr.at[me], 2, t).start()

    for a, b in all_far[SPLIT:]:
        t = dps[a] * n_feat + feats[b]
        send(msg.at[t], rin.at[me], 1, t).start()

    for b in feat_far:
        send(own, ag.at[feat], 3, dp * n_feat + feats[b]).start()

    scr[me] = sc[me]

    arrived(rin.at[pl.ds(0, n_dev - 1)], 1)

    def unpack(b, carry):
        got = rin[pl.ds(b * 16, 16)].astype(f32)
        rows_src[pl.ds(b * 128, 128), :] = jnp.concatenate(
            [got[:, 0:8].reshape(128, 128), got[:, 8:16].reshape(128, 128)], axis=1
        ).astype(bf16)
        return carry

    lax.fori_loop(0, 8, unpack, 0)
    src = iota((8, 1024), 1)
    tag_sel = onehot(((src & 7) == 6) & ((src >> 7) == iota((8, 1024), 0)))
    tags_in = dot(tag_sel, rows_src[...])
    tag_in = (tags_in[:, :128] * 32.0 + tags_in[:, 128:]).astype(i32) - 1
    used = tag_in >= 0
    slot_in = jnp.where(used, tag_in >> 1, -1)
    label_in = jnp.where(used, tag_in & 1, 0)

    def line(x):
        return jnp.concatenate([x[a : a + 1] for a in range(8)], axis=1)

    slot_line = line(slot_in)
    member_line = slot_line >> 6
    spot_line = jnp.where(slot_line < 0, -1, slot_line & 63)
    mine = iota((8, 1024), 0) == member_line
    bhot[...] = onehot((iota((128, 1024), 0) & 63) == spot_line)

    for h in range(4):
        sel = onehot(iota((128, 1024), 0) + 128 * h == slot_line)
        padded[128 * h : 128 * h + 128, :] = dot(sel, rows_src[...]).astype(bf16)

    quarter = iota((16, 128), 1) >> 5
    for m in range(8):
        first = 64 * (m % 2)
        if first == 0:
            pair = padded[64 * m : 64 * m + 128, :]
            prod = dot_nt(pair, pair)
        for h in range(2):
            piece = None
            for r in range(4):
                shift = (32 * r - first - 32 * h) % 128
                lines = prod[first + 16 * r : first + 16 * r + 16]
                lines = pltpu.roll(lines, shift, 1) if shift else lines
                piece = lines if piece is None else jnp.where(quarter == r, lines, piece)
            gram[pl.ds(8 * h + m, 16, stride=16), :] = piece

    marks = jnp.concatenate(
        [jnp.where(mine, line(label_in).astype(f32), 0.0), jnp.where(mine, 1.0, 0.0)], axis=0
    ).astype(bf16)
    marked = dot_nt(marks, bhot[...])
    label, live = marked[0:8], marked[8:16]

    member_of = iota((8, 512), 1) >> 6 == iota((8, 512), 0)
    first = jnp.where(member_of, fold3(dot_nt(stack3(mcoef_ref[...]), padded[...])), 0.0)
    first = (first[:, 0:128] + first[:, 128:256]) + (first[:, 256:384] + first[:, 384:512])
    start = first + pltpu.roll(first, 64, 1)

    arrived(scr.at[pl.ds(0, n_dev - 1)], 2)
    score_in = [jnp.sum(scr[16 * a : 16 * a + 16], axis=0) for a in range(8)]
    score_line = jnp.concatenate(score_in, axis=1)
    offset = fold3(dot_nt(stack3(jnp.where(mine, score_line, 0.0)), bhot[...]))

    lane = iota((8, 128), 1)

    def halves(x):
        return [take(x, (lane & 31) + 32 * h) for h in range(2)]

    def joined(v):
        return jnp.where((lane >> 5) & 1 == 0, v[0], v[1])

    offset, live, label, start = halves(offset), halves(live), halves(label), halves(start)

    def newton(step, carry):
        u = carry[0:2]
        prob = [jax.nn.sigmoid(offset[h] + u[h]) for h in range(2)]
        slope = [live[h] * (prob[h] - label[h]) for h in range(2)]
        root = [jnp.sqrt(live[h] * prob[h] * (1.0 - prob[h])) for h in range(2)]
        pull = gram_times(gram, slope)
        rows = []
        for g in range(16):
            across = by_rows(root, g)
            pair = []
            for h in range(2):
                scaled = gram[16 * g + 8 * h : 16 * g + 8 * h + 8, :] * root[h] * across
                diagonal = 16 * (lane >> 5) + g == 32 * h + (lane & 31)
                pair.append(scaled + jnp.where(diagonal, 1.0, 0.0))
            rows.append(pair)
        solved = solve(rows, [root[h] * (pull[h] + u[h]) for h in range(2)])
        beta = [root[h] * solved[h] - slope[h] for h in range(2)]
        return tuple(gram_times(gram, beta)) + tuple(beta)

    zero = jnp.zeros((8, 128), f32)
    final = lax.fori_loop(0, NEWTON, newton, tuple(start) + (zero, zero))
    value, beta = joined(final[0:2]), joined(final[2:4])

    back = fold3(dot(stack3(jnp.where(lane < 64, value, 0.0)), bhot[...]))
    back = jnp.sum(jnp.where(mine, back, 0.0), axis=0, keepdims=True)
    for a in range(8):
        bk[a] = back[:, 128 * a : 128 * a + 128]

    for a, b in all_far:
        send(bk.at[dps[a]], ret.at[me], 5, dps[a] * n_feat + feats[b]).start()

    ret[me] = bk[dp]

    arrived(ag.at[pl.ds(0, n_feat - 1)], 3)
    scores = jnp.concatenate(
        [ag[f][:, 128 * h : 128 * h + 128] for f in range(n_feat) for h in range(2)], axis=0
    )
    resid = jax.nn.sigmoid(scores + mscore_ref[...]) - click_ref[...].astype(f32)
    grad = jnp.zeros((8, fbuf.shape[1]), f32)
    for b in range(4):
        eight = resid[8 * b : 8 * b + 8]
        wide = jnp.concatenate([eight] * 8, axis=1)
        wide = jnp.where(iota((8, 1024), 1) >> 7 == iota((8, 1024), 0), wide, 0.0).astype(bf16)
        grad = grad + dot(wide, fbuf[1024 * b : 1024 * b + 1024, :])
    gsrc[...] = jnp.sum(grad, axis=0, keepdims=True)

    for a in dp_far:
        send(gsrc, gin.at[dp], 4, dps[a] * n_feat + feat).start()

    gin[dp] = gsrc[...]

    spread = jnp.where(member_of, jnp.concatenate([beta] * 4, axis=1), 0.0)
    out_ref[0:8, :] = fold3(dot(stack3(spread), padded[...]))

    arrived(gin.at[pl.ds(0, n_dp - 1)], 4)
    full = gin[0]
    for t in range(1, n_dp):
        full = full + gin[t]
    full = full / math.sqrt(n_dev * 256)
    out_ref[8:9, :] = full[:, :256]
    out_ref[9:10, :] = full[:, 256:]

    sent(part.at[pl.ds(0, n_feat - 1)], 0)
    sent(msg.at[pl.ds(0, n_dev - 1)], 1)
    sent(sc.at[pl.ds(0, n_dev - 1)], 2)
    sent(ag.at[pl.ds(0, n_feat - 1)], 3)
    sent(gin.at[pl.ds(0, n_dp - 1)], 4)

    arrived(ret.at[pl.ds(0, n_dev - 1)], 5)
    lane_half = onehot(iota((128, 256), 0) == lane_of[...])
    came = ret[...].reshape(n_dev, 128)
    got = [dot(t, lane_half) for t in split3(came)]
    got = (got[0] + got[1]) + got[2]
    mine_back = jnp.sum(jnp.where(iota((n_dev, 256), 0) == slot_ref[...] >> 9, got, 0.0), axis=0)
    out_ref[10:11, :] = own[...] + mine_back[None, :]
    sent(ret.at[pl.ds(0, n_dev - 1)], 5)


def split(merged_ref, grad_ref, coefs_ref, total_ref):
    coefs_ref[...] = merged_ref[0:8, :]
    grad_ref[...] = jnp.concatenate([merged_ref[8:9, :], merged_ref[9:10, :]], axis=1)
    total_ref[...] = merged_ref[10:11, :]


def per_device(
    features, fixed_coef, member_score, clicks, member_features, member_coef, block_slot
):
    n_dev = 128
    rows, width = features.shape
    vmem = pl.BlockSpec(memory_space=pltpu.VMEM)
    merged = pl.pallas_call(
        kernel,
        name="glmix",
        out_shape=pltpu.VMEM((16, 256), f32),
        in_specs=[pl.BlockSpec(memory_space=pltpu.HBM)] * 7,
        out_specs=vmem,
        scratch_shapes=[
            pltpu.VMEM((1, width), f32),
            pltpu.VMEM((rows // 128, 128), f32),
            pltpu.VMEM((rows // 128, 128), i32),
            pltpu.VMEM(member_features.shape, bf16),
            pltpu.VMEM(member_coef.shape, f32),
            pltpu.VMEM((1, 256), i32),
            pltpu.VMEM((rows, width), bf16),
            pltpu.VMEM((n_dev, 16, 128), bf16),
            pltpu.VMEM((n_dev, 16, 128), bf16),
            pltpu.VMEM((16, 1, 256), f32),
            pltpu.VMEM((16, 1, 256), f32),
            pltpu.VMEM((1, 256), f32),
            pltpu.VMEM((16, 1, 256), f32),
            pltpu.VMEM((n_dev, 1, 128), f32),
            pltpu.VMEM((n_dev, 1, 128), f32),
            pltpu.VMEM((8, 1, 128), f32),
            pltpu.VMEM((n_dev, 1, 128), f32),
            pltpu.VMEM((1, width), f32),
            pltpu.VMEM((8, 1, width), f32),
            pltpu.VMEM((n_dev, 256), bf16),
            pltpu.VMEM((1, 256), i32),
            pltpu.VMEM((1024, 256), bf16),
            pltpu.VMEM((128, 1024), bf16),
            pltpu.VMEM((512, 256), bf16),
            pltpu.VMEM((256, 128), f32),
            pltpu.SemaphoreType.DMA((6,)),
            pltpu.SemaphoreType.DMA((8,)),
            pltpu.SemaphoreType.DMA((6,)),
            pltpu.SemaphoreType.DMA((6,)),
        ],
        compiler_params=pltpu.CompilerParams(collective_id=0, has_side_effects=True),
    )(
        fixed_coef.reshape(1, width),
        member_score.reshape(rows // 128, 128),
        clicks.reshape(rows // 128, 128),
        member_features,
        member_coef,
        block_slot.reshape(1, -1),
        features,
    )
    grad, coefs, total = pl.pallas_call(
        split,
        name="split",
        out_shape=(
            jax.ShapeDtypeStruct((1, width), f32),
            jax.ShapeDtypeStruct(member_coef.shape, f32),
            jax.ShapeDtypeStruct((1, block_slot.shape[0]), f32),
        ),
        in_specs=[vmem],
        out_specs=(vmem,) * 3,
        compiler_params=pltpu.CompilerParams(vmem_limit_bytes=1 << 20),
    )(merged)
    return grad.reshape(-1), coefs, total.reshape(-1)


def solution(mesh):
    return jax.shard_map(
        per_device,
        mesh=mesh,
        in_specs=(
            P("dp", "feat"),
            P("feat"),
            P("dp"),
            P("dp"),
            P(("dp", "feat"), None),
            P(("dp", "feat"), None),
            P(("dp", "feat")),
        ),
        out_specs=(P("feat"), P(("dp", "feat"), None), P(("dp", "feat"))),
        check_vma=False,
    )
```

```python
import math

import jax
import jax.numpy as jnp
from jax import lax
from jax.experimental import pallas as pl
from jax.experimental.pallas import tpu as pltpu
from jax.sharding import PartitionSpec as P

SPLIT = 84
LOGICAL = pl.DeviceIdType.LOGICAL
BLK = 64
NEWTON = 3
GROUPS = 2
f32, bf16, i32 = jnp.float32, jnp.bfloat16, jnp.int32


def iota(shape, dim):
    return lax.broadcasted_iota(i32, shape, dim)


def dot(a, b):
    return lax.dot_general(a, b, (((1,), (0,)), ((), ())), preferred_element_type=f32)


def dot_nt(a, b):
    return lax.dot_general(a, b, (((1,), (1,)), ((), ())), preferred_element_type=f32)


def split3(x):
    high = x.astype(bf16)
    rest = x - high.astype(f32)
    mid = rest.astype(bf16)
    low = (rest - mid.astype(f32)).astype(bf16)
    return high, mid, low


def stack3(x):
    return jnp.concatenate([t.astype(f32) for t in split3(x)], axis=0).astype(bf16)


def fold3(y):
    n = y.shape[0] // 3
    return (y[:n] + y[n : 2 * n]) + y[2 * n :]


def onehot(mask):
    return jnp.where(mask, 1.0, 0.0).astype(bf16)


def two_rows(x):
    return jnp.concatenate([x[0:1], x[1:2]], axis=1)


def take(x, index):
    return jnp.take_along_axis(x, index, axis=1, mode="promise_in_bounds")


def solve(rows, y):
    lane = iota((8, 128), 1)
    side = lane & 31
    base = lane - side
    group = lane & 15
    rows = [list(pair) for pair in rows]
    s = [jnp.zeros((8, 128), f32)] * 2
    for q in range(0, 16, GROUPS):
        unknowns = [16 * r + g for r in range(4) for g in range(q, q + GROUPS)]
        n = len(unknowns)

        def at(x, place):
            return jnp.broadcast_to(x[:, place : place + 1], (8, 128))

        block = {}
        for j, v in enumerate(unknowns):
            for i, w in enumerate(unknowns[: j + 1]):
                block[i, j] = at(rows[w % 16][v // 32], 32 * (w // 16) + v % 32)
        ys = [at(y[v // 32], v % 32) for v in unknowns]
        inside = (group >= q) & (group < q + GROUPS)
        done = group < q + GROUPS
        t = []
        for v in unknowns:
            own = [take(rows[v % 16][h], side + 32 * (v // 16)) for h in range(2)]
            own = [jnp.where(inside, 0.0, x) for x in own]
            own[v // 32] = jnp.where(side == v % 32, 1.0, own[v // 32])
            t.append(own)
        inv, factor = [], {}
        for k in range(n):
            inv.append(1.0 / block[k, k])
            for i in range(k + 1, n):
                factor[i, k] = block[k, i] * inv[k]
            for i in range(k + 1, n):
                for j in range(i, n):
                    block[i, j] = block[i, j] - factor[i, k] * block[k, j]
                for h in range(2):
                    t[i][h] = t[i][h] - factor[i, k] * t[k][h]
        for i in range(n):
            t[i] = [x * inv[i] for x in t[i]]
        for k in range(n - 1, 0, -1):
            for i in range(k):
                for h in range(2):
                    t[i][h] = t[i][h] - factor[k, i] * t[k][h]
        step = [tree_sum([ys[i] * t[i][h] for i in range(n)]) for h in range(2)]
        s = [s[h] + jnp.where(done, step[h], 0.0) for h in range(2)]
        y = [y[h] - jnp.where(done, 0.0, step[h]) for h in range(2)]
        for part in (range(q + GROUPS, min(q + 2 * GROUPS, 16)), range(q + 2 * GROUPS, 16)):
            picks = [
                [take(rows[g][v // 32], base + v % 32) for g in part] for v in unknowns
            ]
            for at_, g in enumerate(part):
                for h in range(2):
                    kept = jnp.where(inside, 0.0, rows[g][h])
                    for i in range(n):
                        kept = kept - picks[i][at_] * t[i][h]
                    rows[g][h] = kept
    return s


def tree_sum(terms):
    while len(terms) > 1:
        terms = [sum(terms[i + 1 : i + 2], terms[i]) for i in range(0, len(terms), 2)]
    return terms[0]


def by_rows(v, g):
    lane = iota((8, 128), 1)
    r = lane >> 5
    return take(jnp.where(lane < 64, v[0], v[1]), 32 * r + 16 * (r & 1) + g)


def gram_times(gram_ref, v):
    picks = [by_rows(v, g) for g in range(16)]
    out = []
    for h in range(2):
        total = tree_sum(
            [gram_ref[16 * g + 8 * h : 16 * g + 8 * h + 8, :] * picks[g] for g in range(16)]
        )
        turns = [pltpu.roll(total, shift, 1) for shift in (32, 64, 96)]
        out.append((total + turns[0]) + (turns[1] + turns[2]))
    return out


def kernel(
    coef_hbm, mscore_hbm, click_hbm, mfeat_hbm, mcoef_hbm, slot_hbm, feat_ref,
    out_ref,
    coef_ref, mscore_ref, click_ref, mfeat_ref, mcoef_ref, slot_ref,
    fbuf, msg, rin, part, rs, own, ag, sc, scr, bk, ret, gsrc, gin,
    owner_hot, lane_of, rows_src, bhot, padded, gram,
    isem, fsem, ssem, rsem,
):
    n_dp, n_feat = 8, 16
    n_dev = n_dp * n_feat
    dp, feat = lax.axis_index("dp"), lax.axis_index("feat")
    me = dp * n_feat + feat

    chunks = 8
    rows_chunk = fbuf.shape[0] // chunks

    def feature_copy(c):
        window = pl.ds(c * rows_chunk, rows_chunk)
        return pltpu.make_async_copy(feat_ref.at[window], fbuf.at[window], fsem.at[c])

    loads = [
        pltpu.make_async_copy(src, dst, isem.at[i])
        for i, (src, dst) in enumerate([
            (slot_hbm, slot_ref), (click_hbm, click_ref), (mfeat_hbm, mfeat_ref),
            (coef_hbm, coef_ref), (mscore_hbm, mscore_ref), (mcoef_hbm, mcoef_ref),
        ])
    ]
    for load in loads:
        load.start()
    for c in range(chunks):
        feature_copy(c).start()

    barrier = pltpu.get_barrier_semaphore()

    dps = [2 * lax.rem(dp // 2 + dy, 4) + lax.rem(dp + dc, 2) for dy in range(4) for dc in range(2)]
    feats = [
        4 * lax.rem(feat // 4 + dz, 4) + lax.rem(feat + dx, 4) for dz in range(4) for dx in range(4)
    ]
    hops = [0, 1, 2, 1]
    dp_far = sorted(range(1, 8), key=lambda a: -hops[a // 2])
    feat_far = sorted(range(1, 16), key=lambda b: -hops[b // 4] - hops[b % 4])
    all_far = sorted(
        ((a, b) for a in range(8) for b in range(16) if a or b),
        key=lambda ab: -hops[ab[0] // 2] - hops[ab[1] // 4] - hops[ab[1] % 4],
    )

    for a, b in all_far:
        pl.semaphore_signal(
            barrier, inc=1, device_id=dps[a] * n_feat + feats[b], device_id_type=LOGICAL
        )

    def send(src, dst, which, target):
        return pltpu.make_async_remote_copy(
            src_ref=src, dst_ref=dst, send_sem=ssem.at[which], recv_sem=rsem.at[which],
            device_id=target, device_id_type=LOGICAL,
        )

    def arrived(ref, which):
        send(ref, ref, which, me).wait_recv()

    def sent(ref, which):
        send(ref, ref, which, me).wait_send()

    for load in loads:
        load.wait()
    slots = slot_ref[...]
    owner = slots >> 9
    own_clicks = two_rows(click_ref[pl.ds(2 * feat, 2), :])
    tag = (slots & 511) * 2 + own_clicks + 1
    hot = iota((n_dev, 256), 0) == owner
    hot_half = onehot(hot)
    before = onehot(iota((256, 256), 0) < iota((256, 256), 1))
    counts = dot(hot_half, before)
    rank = jnp.sum(jnp.where(hot, counts, 0.0), axis=0, keepdims=True).astype(i32)
    lane_row = rank + feat * 8
    owner_hot[...] = hot_half
    lane_of[...] = lane_row
    place = owner * 8 + rank
    lane_hot = iota((128, 256), 0) == lane_row

    def by_owner(row):
        return dot_nt(hot_half, jnp.where(lane_hot, row, 0.0).astype(bf16))

    tags = jnp.concatenate(
        [by_owner((tag >> 5).astype(f32)), by_owner((tag & 31).astype(f32))], axis=1
    ).astype(bf16)

    def pack(b, carry):
        base = b * 128
        sel = onehot(iota((128, 256), 0) + base == place)
        extra = onehot(iota((128, 128), 0) + base == iota((128, 128), 1) * 8 + 6)
        out = dot(sel, mfeat_ref[...]) + dot(extra, tags)
        msg[pl.ds(b * 16, 16)] = jnp.concatenate(
            [out[:, :128].reshape(16, 8, 128), out[:, 128:].reshape(16, 8, 128)], axis=1
        ).astype(bf16)
        return carry

    for b in range(8):
        pack(b, 0)

    coef = jnp.broadcast_to(coef_ref[...], (8, coef_ref.shape[1])).astype(bf16)
    for c in range(chunks):
        feature_copy(c).wait()
        out = dot_nt(coef, fbuf[c * rows_chunk : (c + 1) * rows_chunk, :])[0:1]
        for j in range(rows_chunk // 256):
            part[c * (rows_chunk // 256) + j] = out[:, 256 * j : 256 * j + 256]

    pl.semaphore_wait(barrier, n_dev - 1)

    for b in feat_far:
        send(part.at[feats[b]], rs.at[feat], 0, dp * n_feat + feats[b]).start()

    for a, b in all_far[:SPLIT]:
        t = dps[a] * n_feat + feats[b]
        send(msg.at[t], rin.at[me], 1, t).start()

    rs[feat] = part[feat]
    rin[me] = msg[me]

    arrived(rs.at[pl.ds(0, n_feat - 1)], 0)
    for a, b in all_far[SPLIT:105]:
        t = dps[a] * n_feat + feats[b]
        send(msg.at[t], rin.at[me], 1, t).start()

    score = rs[0]
    for f in range(1, n_feat):
        score = score + rs[f]
    own[...] = score
    ag[feat] = score
    lane_hot = iota((128, 256), 0) == lane_of[...]
    parts = [
        dot_nt(owner_hot[...], jnp.where(lane_hot, t.astype(f32), 0.0).astype(bf16))
        for t in split3(score)
    ]
    by = (parts[0] + parts[1]) + parts[2]
    sc[...] = by.reshape(n_dev, 1, 128)

    for a, b in all_far:
        t = dps[a] * n_feat + feats[b]
        send(sc.at[t], scr.at[me], 2, t).start()

    for a, b in all_far[105:]:
        t = dps[a] * n_feat + feats[b]
        send(msg.at[t], rin.at[me], 1, t).start()

    for b in feat_far:
        send(own, ag.at[feat], 3, dp * n_feat + feats[b]).start()

    scr[me] = sc[me]

    arrived(rin.at[pl.ds(0, n_dev - 1)], 1)

    def unpack(b, carry):
        got = rin[pl.ds(b * 16, 16)].astype(f32)
        rows_src[pl.ds(b * 128, 128), :] = jnp.concatenate(
            [got[:, 0:8].reshape(128, 128), got[:, 8:16].reshape(128, 128)], axis=1
        ).astype(bf16)
        return carry

    lax.fori_loop(0, 8, unpack, 0)
    src = iota((8, 1024), 1)
    tag_sel = onehot(((src & 7) == 6) & ((src >> 7) == iota((8, 1024), 0)))
    tags_in = dot(tag_sel, rows_src[...])
    tag_in = (tags_in[:, :128] * 32.0 + tags_in[:, 128:]).astype(i32) - 1
    used = tag_in >= 0
    slot_in = jnp.where(used, tag_in >> 1, -1)
    label_in = jnp.where(used, tag_in & 1, 0)

    def line(x):
        return jnp.concatenate([x[a : a + 1] for a in range(8)], axis=1)

    slot_line = line(slot_in)
    member_line = slot_line >> 6
    spot_line = jnp.where(slot_line < 0, -1, slot_line & 63)
    mine = iota((8, 1024), 0) == member_line
    bhot[...] = onehot((iota((128, 1024), 0) & 63) == spot_line)

    for h in range(4):
        sel = onehot(iota((128, 1024), 0) + 128 * h == slot_line)
        padded[128 * h : 128 * h + 128, :] = dot(sel, rows_src[...]).astype(bf16)

    quarter = iota((16, 128), 1) >> 5
    for m in range(8):
        first = 64 * (m % 2)
        if first == 0:
            pair = padded[64 * m : 64 * m + 128, :]
            prod = dot_nt(pair, pair)
        for h in range(2):
            piece = None
            for r in range(4):
                shift = (32 * r - first - 32 * h) % 128
                lines = prod[first + 16 * r : first + 16 * r + 16]
                lines = pltpu.roll(lines, shift, 1) if shift else lines
                piece = lines if piece is None else jnp.where(quarter == r, lines, piece)
            gram[pl.ds(8 * h + m, 16, stride=16), :] = piece

    marks = jnp.concatenate(
        [jnp.where(mine, line(label_in).astype(f32), 0.0), jnp.where(mine, 1.0, 0.0)], axis=0
    ).astype(bf16)
    marked = dot_nt(marks, bhot[...])
    label, live = marked[0:8], marked[8:16]

    member_of = iota((8, 512), 1) >> 6 == iota((8, 512), 0)
    first = jnp.where(member_of, fold3(dot_nt(stack3(mcoef_ref[...]), padded[...])), 0.0)
    first = (first[:, 0:128] + first[:, 128:256]) + (first[:, 256:384] + first[:, 384:512])
    start = first + pltpu.roll(first, 64, 1)

    arrived(scr.at[pl.ds(0, n_dev - 1)], 2)
    score_in = [jnp.sum(scr[16 * a : 16 * a + 16], axis=0) for a in range(8)]
    score_line = jnp.concatenate(score_in, axis=1)
    offset = fold3(dot_nt(stack3(jnp.where(mine, score_line, 0.0)), bhot[...]))

    lane = iota((8, 128), 1)

    def halves(x):
        return [take(x, (lane & 31) + 32 * h) for h in range(2)]

    def joined(v):
        return jnp.where((lane >> 5) & 1 == 0, v[0], v[1])

    offset, live, label, start = halves(offset), halves(live), halves(label), halves(start)

    def newton(step, carry):
        u = carry[0:2]
        prob = [jax.nn.sigmoid(offset[h] + u[h]) for h in range(2)]
        slope = [live[h] * (prob[h] - label[h]) for h in range(2)]
        root = [jnp.sqrt(live[h] * prob[h] * (1.0 - prob[h])) for h in range(2)]
        pull = gram_times(gram, slope)
        rows = []
        for g in range(16):
            across = by_rows(root, g)
            pair = []
            for h in range(2):
                scaled = gram[16 * g + 8 * h : 16 * g + 8 * h + 8, :] * root[h] * across
                diagonal = 16 * (lane >> 5) + g == 32 * h + (lane & 31)
                pair.append(scaled + jnp.where(diagonal, 1.0, 0.0))
            rows.append(pair)
        solved = solve(rows, [root[h] * (pull[h] + u[h]) for h in range(2)])
        beta = [root[h] * solved[h] - slope[h] for h in range(2)]
        return tuple(gram_times(gram, beta)) + tuple(beta)

    zero = jnp.zeros((8, 128), f32)
    final = lax.fori_loop(0, NEWTON, newton, tuple(start) + (zero, zero))
    value, beta = joined(final[0:2]), joined(final[2:4])

    back = fold3(dot(stack3(jnp.where(lane < 64, value, 0.0)), bhot[...]))
    back = jnp.sum(jnp.where(mine, back, 0.0), axis=0, keepdims=True)
    for a in range(8):
        bk[a] = back[:, 128 * a : 128 * a + 128]

    for a, b in all_far:
        send(bk.at[dps[a]], ret.at[me], 5, dps[a] * n_feat + feats[b]).start()

    ret[me] = bk[dp]

    arrived(ag.at[pl.ds(0, n_feat - 1)], 3)
    scores = jnp.concatenate(
        [ag[f][:, 128 * h : 128 * h + 128] for f in range(n_feat) for h in range(2)], axis=0
    )
    resid = jax.nn.sigmoid(scores + mscore_ref[...]) - click_ref[...].astype(f32)
    grad = jnp.zeros((8, fbuf.shape[1]), f32)
    for b in range(4):
        eight = resid[8 * b : 8 * b + 8]
        wide = jnp.concatenate([eight] * 8, axis=1)
        wide = jnp.where(iota((8, 1024), 1) >> 7 == iota((8, 1024), 0), wide, 0.0).astype(bf16)
        grad = grad + dot(wide, fbuf[1024 * b : 1024 * b + 1024, :])
    gsrc[...] = jnp.sum(grad, axis=0, keepdims=True)

    for a in dp_far:
        send(gsrc, gin.at[dp], 4, dps[a] * n_feat + feat).start()

    gin[dp] = gsrc[...]

    spread = jnp.where(member_of, jnp.concatenate([beta] * 4, axis=1), 0.0)
    out_ref[0:8, :] = fold3(dot(stack3(spread), padded[...]))

    arrived(gin.at[pl.ds(0, n_dp - 1)], 4)
    full = gin[0]
    for t in range(1, n_dp):
        full = full + gin[t]
    full = full / math.sqrt(n_dev * 256)
    out_ref[8:9, :] = full[:, :256]
    out_ref[9:10, :] = full[:, 256:]

    sent(part.at[pl.ds(0, n_feat - 1)], 0)
    sent(msg.at[pl.ds(0, n_dev - 1)], 1)
    sent(sc.at[pl.ds(0, n_dev - 1)], 2)
    sent(ag.at[pl.ds(0, n_feat - 1)], 3)
    sent(gin.at[pl.ds(0, n_dp - 1)], 4)

    arrived(ret.at[pl.ds(0, n_dev - 1)], 5)
    lane_half = onehot(iota((128, 256), 0) == lane_of[...])
    came = ret[...].reshape(n_dev, 128)
    got = dot(jnp.concatenate(split3(came), axis=1), jnp.concatenate([lane_half] * 3, axis=0))
    mine_back = jnp.sum(jnp.where(iota((n_dev, 256), 0) == slot_ref[...] >> 9, got, 0.0), axis=0)
    out_ref[10:11, :] = own[...] + mine_back[None, :]
    sent(ret.at[pl.ds(0, n_dev - 1)], 5)


def split(merged_ref, grad_ref, coefs_ref, total_ref):
    coefs_ref[...] = merged_ref[0:8, :]
    grad_ref[...] = jnp.concatenate([merged_ref[8:9, :], merged_ref[9:10, :]], axis=1)
    total_ref[...] = merged_ref[10:11, :]


def per_device(
    features, fixed_coef, member_score, clicks, member_features, member_coef, block_slot
):
    n_dev = 128
    rows, width = features.shape
    vmem = pl.BlockSpec(memory_space=pltpu.VMEM)
    merged = pl.pallas_call(
        kernel,
        name="glmix",
        out_shape=pltpu.VMEM((16, 256), f32),
        in_specs=[pl.BlockSpec(memory_space=pltpu.HBM)] * 7,
        out_specs=vmem,
        scratch_shapes=[
            pltpu.VMEM((1, width), f32),
            pltpu.VMEM((rows // 128, 128), f32),
            pltpu.VMEM((rows // 128, 128), i32),
            pltpu.VMEM(member_features.shape, bf16),
            pltpu.VMEM(member_coef.shape, f32),
            pltpu.VMEM((1, 256), i32),
            pltpu.VMEM((rows, width), bf16),
            pltpu.VMEM((n_dev, 16, 128), bf16),
            pltpu.VMEM((n_dev, 16, 128), bf16),
            pltpu.VMEM((16, 1, 256), f32),
            pltpu.VMEM((16, 1, 256), f32),
            pltpu.VMEM((1, 256), f32),
            pltpu.VMEM((16, 1, 256), f32),
            pltpu.VMEM((n_dev, 1, 128), f32),
            pltpu.VMEM((n_dev, 1, 128), f32),
            pltpu.VMEM((8, 1, 128), f32),
            pltpu.VMEM((n_dev, 1, 128), f32),
            pltpu.VMEM((1, width), f32),
            pltpu.VMEM((8, 1, width), f32),
            pltpu.VMEM((n_dev, 256), bf16),
            pltpu.VMEM((1, 256), i32),
            pltpu.VMEM((1024, 256), bf16),
            pltpu.VMEM((128, 1024), bf16),
            pltpu.VMEM((512, 256), bf16),
            pltpu.VMEM((256, 128), f32),
            pltpu.SemaphoreType.DMA((6,)),
            pltpu.SemaphoreType.DMA((8,)),
            pltpu.SemaphoreType.DMA((6,)),
            pltpu.SemaphoreType.DMA((6,)),
        ],
        compiler_params=pltpu.CompilerParams(collective_id=0, has_side_effects=True),
    )(
        fixed_coef.reshape(1, width),
        member_score.reshape(rows // 128, 128),
        clicks.reshape(rows // 128, 128),
        member_features,
        member_coef,
        block_slot.reshape(1, -1),
        features,
    )
    grad, coefs, total = pl.pallas_call(
        split,
        name="split",
        out_shape=(
            jax.ShapeDtypeStruct((1, width), f32),
            jax.ShapeDtypeStruct(member_coef.shape, f32),
            jax.ShapeDtypeStruct((1, block_slot.shape[0]), f32),
        ),
        in_specs=[vmem],
        out_specs=(vmem,) * 3,
        compiler_params=pltpu.CompilerParams(vmem_limit_bytes=1 << 20),
    )(merged)
    return grad.reshape(-1), coefs, total.reshape(-1)


def solution(mesh):
    return jax.shard_map(
        per_device,
        mesh=mesh,
        in_specs=(
            P("dp", "feat"),
            P("feat"),
            P("dp"),
            P("dp"),
            P(("dp", "feat"), None),
            P(("dp", "feat"), None),
            P(("dp", "feat")),
        ),
        out_specs=(P("feat"), P(("dp", "feat"), None), P(("dp", "feat"))),
        check_vma=False,
    )
```

```python
import math

import jax
import jax.numpy as jnp
from jax import lax
from jax.experimental import pallas as pl
from jax.experimental.pallas import tpu as pltpu
from jax.sharding import PartitionSpec as P

SPLIT = 84
LOGICAL = pl.DeviceIdType.LOGICAL
BLK = 64
NEWTON = 3
GROUPS = 2
f32, bf16, i32 = jnp.float32, jnp.bfloat16, jnp.int32


def iota(shape, dim):
    return lax.broadcasted_iota(i32, shape, dim)


def dot(a, b):
    return lax.dot_general(a, b, (((1,), (0,)), ((), ())), preferred_element_type=f32)


def dot_nt(a, b):
    return lax.dot_general(a, b, (((1,), (1,)), ((), ())), preferred_element_type=f32)


def split3(x):
    high = x.astype(bf16)
    rest = x - high.astype(f32)
    mid = rest.astype(bf16)
    low = (rest - mid.astype(f32)).astype(bf16)
    return high, mid, low


def stack3(x):
    return jnp.concatenate([t.astype(f32) for t in split3(x)], axis=0).astype(bf16)


def fold3(y):
    n = y.shape[0] // 3
    return (y[:n] + y[n : 2 * n]) + y[2 * n :]


def onehot(mask):
    return jnp.where(mask, 1.0, 0.0).astype(bf16)


def two_rows(x):
    return jnp.concatenate([x[0:1], x[1:2]], axis=1)


def take(x, index):
    return jnp.take_along_axis(x, index, axis=1, mode="promise_in_bounds")


def solve(rows, y):
    lane = iota((8, 128), 1)
    side = lane & 31
    base = lane - side
    group = lane & 15
    rows = [list(pair) for pair in rows]
    s = [jnp.zeros((8, 128), f32)] * 2
    for q in range(0, 16, GROUPS):
        unknowns = [16 * r + g for r in range(4) for g in range(q, q + GROUPS)]
        n = len(unknowns)

        def at(x, place):
            return jnp.broadcast_to(x[:, place : place + 1], (8, 128))

        block = {}
        for j, v in enumerate(unknowns):
            for i, w in enumerate(unknowns[: j + 1]):
                block[i, j] = at(rows[w % 16][v // 32], 32 * (w // 16) + v % 32)
        ys = [at(y[v // 32], v % 32) for v in unknowns]
        inside = (group >= q) & (group < q + GROUPS)
        done = group < q + GROUPS
        t = []
        for v in unknowns:
            own = [take(rows[v % 16][h], side + 32 * (v // 16)) for h in range(2)]
            own = [jnp.where(inside, 0.0, x) for x in own]
            own[v // 32] = jnp.where(side == v % 32, 1.0, own[v // 32])
            t.append(own)
        inv, factor = [], {}
        for k in range(n):
            inv.append(1.0 / block[k, k])
            for i in range(k + 1, n):
                factor[i, k] = block[k, i] * inv[k]
            for i in range(k + 1, n):
                for j in range(i, n):
                    block[i, j] = block[i, j] - factor[i, k] * block[k, j]
                for h in range(2):
                    t[i][h] = t[i][h] - factor[i, k] * t[k][h]
        for i in range(n):
            t[i] = [x * inv[i] for x in t[i]]
        for k in range(n - 1, 0, -1):
            for i in range(k):
                for h in range(2):
                    t[i][h] = t[i][h] - factor[k, i] * t[k][h]
        step = [tree_sum([ys[i] * t[i][h] for i in range(n)]) for h in range(2)]
        if q + GROUPS == 16:
            return [s[h] + step[h] for h in range(2)]
        s = [s[h] + jnp.where(done, step[h], 0.0) for h in range(2)]
        y = [y[h] - jnp.where(done, 0.0, step[h]) for h in range(2)]
        for part in (range(q + GROUPS, min(q + 2 * GROUPS, 16)), range(q + 2 * GROUPS, 16)):
            picks = [
                [take(rows[g][v // 32], base + v % 32) for g in part] for v in unknowns
            ]
            for at_, g in enumerate(part):
                for h in range(2):
                    kept = jnp.where(inside, 0.0, rows[g][h])
                    for i in range(n):
                        kept = kept - picks[i][at_] * t[i][h]
                    rows[g][h] = kept


def tree_sum(terms):
    while len(terms) > 1:
        terms = [sum(terms[i + 1 : i + 2], terms[i]) for i in range(0, len(terms), 2)]
    return terms[0]


def by_rows(v, g):
    lane = iota((8, 128), 1)
    r = lane >> 5
    return take(jnp.where(lane < 64, v[0], v[1]), 32 * r + 16 * (r & 1) + g)


def gram_times(gram_ref, v):
    picks = [by_rows(v, g) for g in range(16)]
    out = []
    for h in range(2):
        total = tree_sum(
            [gram_ref[16 * g + 8 * h : 16 * g + 8 * h + 8, :] * picks[g] for g in range(16)]
        )
        turns = [pltpu.roll(total, shift, 1) for shift in (32, 64, 96)]
        out.append((total + turns[0]) + (turns[1] + turns[2]))
    return out


def kernel(
    coef_hbm, mscore_hbm, click_hbm, mfeat_hbm, mcoef_hbm, slot_hbm, feat_ref,
    out_ref,
    coef_ref, mscore_ref, click_ref, mfeat_ref, mcoef_ref, slot_ref,
    fbuf, msg, rin, part, rs, own, ag, sc, scr, bk, ret, gsrc, gin,
    owner_hot, lane_of, rows_src, bhot, padded, gram,
    isem, fsem, ssem, rsem,
):
    n_dp, n_feat = 8, 16
    n_dev = n_dp * n_feat
    dp, feat = lax.axis_index("dp"), lax.axis_index("feat")
    me = dp * n_feat + feat

    chunks = 8
    rows_chunk = fbuf.shape[0] // chunks

    def feature_copy(c):
        window = pl.ds(c * rows_chunk, rows_chunk)
        return pltpu.make_async_copy(feat_ref.at[window], fbuf.at[window], fsem.at[c])

    loads = [
        pltpu.make_async_copy(src, dst, isem.at[i])
        for i, (src, dst) in enumerate([
            (slot_hbm, slot_ref), (click_hbm, click_ref), (mfeat_hbm, mfeat_ref),
            (coef_hbm, coef_ref), (mscore_hbm, mscore_ref), (mcoef_hbm, mcoef_ref),
        ])
    ]
    for load in loads:
        load.start()
    for c in range(chunks):
        feature_copy(c).start()

    barrier = pltpu.get_barrier_semaphore()

    dps = [2 * lax.rem(dp // 2 + dy, 4) + lax.rem(dp + dc, 2) for dy in range(4) for dc in range(2)]
    feats = [
        4 * lax.rem(feat // 4 + dz, 4) + lax.rem(feat + dx, 4) for dz in range(4) for dx in range(4)
    ]
    hops = [0, 1, 2, 1]
    dp_far = sorted(range(1, 8), key=lambda a: -hops[a // 2])
    feat_far = sorted(range(1, 16), key=lambda b: -hops[b // 4] - hops[b % 4])
    all_far = sorted(
        ((a, b) for a in range(8) for b in range(16) if a or b),
        key=lambda ab: -hops[ab[0] // 2] - hops[ab[1] // 4] - hops[ab[1] % 4],
    )

    for a, b in all_far:
        pl.semaphore_signal(
            barrier, inc=1, device_id=dps[a] * n_feat + feats[b], device_id_type=LOGICAL
        )

    def send(src, dst, which, target):
        return pltpu.make_async_remote_copy(
            src_ref=src, dst_ref=dst, send_sem=ssem.at[which], recv_sem=rsem.at[which],
            device_id=target, device_id_type=LOGICAL,
        )

    def arrived(ref, which):
        send(ref, ref, which, me).wait_recv()

    def sent(ref, which):
        send(ref, ref, which, me).wait_send()

    for load in loads:
        load.wait()
    slots = slot_ref[...]
    owner = slots >> 9
    own_clicks = two_rows(click_ref[pl.ds(2 * feat, 2), :])
    tag = (slots & 511) * 2 + own_clicks + 1
    hot = iota((n_dev, 256), 0) == owner
    hot_half = onehot(hot)
    before = onehot(iota((256, 256), 0) < iota((256, 256), 1))
    counts = dot(hot_half, before)
    rank = jnp.sum(jnp.where(hot, counts, 0.0), axis=0, keepdims=True).astype(i32)
    lane_row = rank + feat * 8
    owner_hot[...] = hot_half
    lane_of[...] = lane_row
    place = owner * 8 + rank
    lane_hot = iota((128, 256), 0) == lane_row

    def by_owner(row):
        return dot_nt(hot_half, jnp.where(lane_hot, row, 0.0).astype(bf16))

    tags = jnp.concatenate(
        [by_owner((tag >> 5).astype(f32)), by_owner((tag & 31).astype(f32))], axis=1
    ).astype(bf16)

    def pack(b, carry):
        base = b * 128
        sel = onehot(iota((128, 256), 0) + base == place)
        extra = onehot(iota((128, 128), 0) + base == iota((128, 128), 1) * 8 + 6)
        out = dot(sel, mfeat_ref[...]) + dot(extra, tags)
        msg[pl.ds(b * 16, 16)] = jnp.concatenate(
            [out[:, :128].reshape(16, 8, 128), out[:, 128:].reshape(16, 8, 128)], axis=1
        ).astype(bf16)
        return carry

    for b in range(8):
        pack(b, 0)

    coef = jnp.broadcast_to(coef_ref[...], (8, coef_ref.shape[1])).astype(bf16)
    for c in range(chunks):
        feature_copy(c).wait()
        out = dot_nt(coef, fbuf[c * rows_chunk : (c + 1) * rows_chunk, :])[0:1]
        for j in range(rows_chunk // 256):
            part[c * (rows_chunk // 256) + j] = out[:, 256 * j : 256 * j + 256]

    pl.semaphore_wait(barrier, n_dev - 1)

    for b in feat_far:
        send(part.at[feats[b]], rs.at[feat], 0, dp * n_feat + feats[b]).start()

    for a, b in all_far[:SPLIT]:
        t = dps[a] * n_feat + feats[b]
        send(msg.at[t], rin.at[me], 1, t).start()

    rs[feat] = part[feat]
    rin[me] = msg[me]

    arrived(rs.at[pl.ds(0, n_feat - 1)], 0)
    for a, b in all_far[SPLIT:105]:
        t = dps[a] * n_feat + feats[b]
        send(msg.at[t], rin.at[me], 1, t).start()

    score = tree_sum([rs[f] for f in range(n_feat)])
    own[...] = score
    ag[feat] = score
    lane_hot = iota((128, 256), 0) == lane_of[...]
    parts = [
        dot_nt(owner_hot[...], jnp.where(lane_hot, t.astype(f32), 0.0).astype(bf16))
        for t in split3(score)
    ]
    by = (parts[0] + parts[1]) + parts[2]
    sc[...] = by.reshape(n_dev, 1, 128)

    for a, b in all_far:
        t = dps[a] * n_feat + feats[b]
        send(sc.at[t], scr.at[me], 2, t).start()

    for a, b in all_far[105:]:
        t = dps[a] * n_feat + feats[b]
        send(msg.at[t], rin.at[me], 1, t).start()

    for b in feat_far:
        send(own, ag.at[feat], 3, dp * n_feat + feats[b]).start()

    scr[me] = sc[me]

    arrived(rin.at[pl.ds(0, n_dev - 1)], 1)

    def unpack(b, carry):
        got = rin[pl.ds(b * 16, 16)].astype(f32)
        rows_src[pl.ds(b * 128, 128), :] = jnp.concatenate(
            [got[:, 0:8].reshape(128, 128), got[:, 8:16].reshape(128, 128)], axis=1
        ).astype(bf16)
        return carry

    lax.fori_loop(0, 8, unpack, 0)
    src = iota((8, 1024), 1)
    tag_sel = onehot(((src & 7) == 6) & ((src >> 7) == iota((8, 1024), 0)))
    tags_in = dot(tag_sel, rows_src[...])
    tag_in = (tags_in[:, :128] * 32.0 + tags_in[:, 128:]).astype(i32) - 1
    used = tag_in >= 0
    slot_in = jnp.where(used, tag_in >> 1, -1)
    label_in = jnp.where(used, tag_in & 1, 0)

    def line(x):
        return jnp.concatenate([x[a : a + 1] for a in range(8)], axis=1)

    slot_line = line(slot_in)
    member_line = slot_line >> 6
    spot_line = jnp.where(slot_line < 0, -1, slot_line & 63)
    mine = iota((8, 1024), 0) == member_line
    bhot[...] = onehot((iota((128, 1024), 0) & 63) == spot_line)

    for h in range(4):
        sel = onehot(iota((128, 1024), 0) + 128 * h == slot_line)
        padded[128 * h : 128 * h + 128, :] = dot(sel, rows_src[...]).astype(bf16)

    quarter = iota((16, 128), 1) >> 5
    for m in range(8):
        first = 64 * (m % 2)
        if first == 0:
            pair = padded[64 * m : 64 * m + 128, :]
            prod = dot_nt(pair, pair)
        for h in range(2):
            piece = None
            for r in range(4):
                shift = (32 * r - first - 32 * h) % 128
                lines = prod[first + 16 * r : first + 16 * r + 16]
                lines = pltpu.roll(lines, shift, 1) if shift else lines
                piece = lines if piece is None else jnp.where(quarter == r, lines, piece)
            gram[pl.ds(8 * h + m, 16, stride=16), :] = piece

    marks = jnp.concatenate(
        [jnp.where(mine, line(label_in).astype(f32), 0.0), jnp.where(mine, 1.0, 0.0)], axis=0
    ).astype(bf16)
    marked = dot_nt(marks, bhot[...])
    label, live = marked[0:8], marked[8:16]

    member_of = iota((8, 512), 1) >> 6 == iota((8, 512), 0)
    first = jnp.where(member_of, fold3(dot_nt(stack3(mcoef_ref[...]), padded[...])), 0.0)
    first = (first[:, 0:128] + first[:, 128:256]) + (first[:, 256:384] + first[:, 384:512])
    start = first + pltpu.roll(first, 64, 1)

    arrived(scr.at[pl.ds(0, n_dev - 1)], 2)
    score_in = [jnp.sum(scr[16 * a : 16 * a + 16], axis=0) for a in range(8)]
    score_line = jnp.concatenate(score_in, axis=1)
    offset = fold3(dot_nt(stack3(jnp.where(mine, score_line, 0.0)), bhot[...]))

    lane = iota((8, 128), 1)

    def halves(x):
        return [take(x, (lane & 31) + 32 * h) for h in range(2)]

    def joined(v):
        return jnp.where((lane >> 5) & 1 == 0, v[0], v[1])

    offset, live, label, start = halves(offset), halves(live), halves(label), halves(start)

    def newton(step, carry):
        u = carry[0:2]
        prob = [jax.nn.sigmoid(offset[h] + u[h]) for h in range(2)]
        slope = [live[h] * (prob[h] - label[h]) for h in range(2)]
        root = [jnp.sqrt(live[h] * prob[h] * (1.0 - prob[h])) for h in range(2)]
        pull = gram_times(gram, slope)
        rows = []
        for g in range(16):
            across = by_rows(root, g)
            pair = []
            for h in range(2):
                scaled = gram[16 * g + 8 * h : 16 * g + 8 * h + 8, :] * root[h] * across
                diagonal = 16 * (lane >> 5) + g == 32 * h + (lane & 31)
                pair.append(scaled + jnp.where(diagonal, 1.0, 0.0))
            rows.append(pair)
        solved = solve(rows, [root[h] * (pull[h] + u[h]) for h in range(2)])
        beta = [root[h] * solved[h] - slope[h] for h in range(2)]
        return tuple(gram_times(gram, beta)) + tuple(beta)

    zero = jnp.zeros((8, 128), f32)
    final = lax.fori_loop(0, NEWTON, newton, tuple(start) + (zero, zero))
    value, beta = joined(final[0:2]), joined(final[2:4])

    back = fold3(dot(stack3(jnp.where(lane < 64, value, 0.0)), bhot[...]))
    back = jnp.sum(jnp.where(mine, back, 0.0), axis=0, keepdims=True)
    for a in range(8):
        bk[a] = back[:, 128 * a : 128 * a + 128]

    for a, b in all_far:
        send(bk.at[dps[a]], ret.at[me], 5, dps[a] * n_feat + feats[b]).start()

    ret[me] = bk[dp]

    arrived(ag.at[pl.ds(0, n_feat - 1)], 3)
    scores = jnp.concatenate(
        [ag[f][:, 128 * h : 128 * h + 128] for f in range(n_feat) for h in range(2)], axis=0
    )
    resid = jax.nn.sigmoid(scores + mscore_ref[...]) - click_ref[...].astype(f32)
    grad = jnp.zeros((8, fbuf.shape[1]), f32)
    for b in range(4):
        eight = resid[8 * b : 8 * b + 8]
        wide = jnp.concatenate([eight] * 8, axis=1)
        wide = jnp.where(iota((8, 1024), 1) >> 7 == iota((8, 1024), 0), wide, 0.0).astype(bf16)
        grad = grad + dot(wide, fbuf[1024 * b : 1024 * b + 1024, :])
    gsrc[...] = jnp.sum(grad, axis=0, keepdims=True)

    for a in dp_far:
        send(gsrc, gin.at[dp], 4, dps[a] * n_feat + feat).start()

    gin[dp] = gsrc[...]

    spread = jnp.where(member_of, jnp.concatenate([beta] * 4, axis=1), 0.0)
    out_ref[0:8, :] = fold3(dot(stack3(spread), padded[...]))

    arrived(gin.at[pl.ds(0, n_dp - 1)], 4)
    full = gin[0]
    for t in range(1, n_dp):
        full = full + gin[t]
    full = full / math.sqrt(n_dev * 256)
    out_ref[8:9, :] = full[:, :256]
    out_ref[9:10, :] = full[:, 256:]

    sent(part.at[pl.ds(0, n_feat - 1)], 0)
    sent(msg.at[pl.ds(0, n_dev - 1)], 1)
    sent(sc.at[pl.ds(0, n_dev - 1)], 2)
    sent(ag.at[pl.ds(0, n_feat - 1)], 3)
    sent(gin.at[pl.ds(0, n_dp - 1)], 4)

    arrived(ret.at[pl.ds(0, n_dev - 1)], 5)
    lane_half = onehot(iota((128, 256), 0) == lane_of[...])
    came = ret[...].reshape(n_dev, 128)
    got = dot(jnp.concatenate(split3(came), axis=1), jnp.concatenate([lane_half] * 3, axis=0))
    mine_back = jnp.sum(jnp.where(iota((n_dev, 256), 0) == slot_ref[...] >> 9, got, 0.0), axis=0)
    out_ref[10:11, :] = own[...] + mine_back[None, :]
    sent(ret.at[pl.ds(0, n_dev - 1)], 5)


def split(merged_ref, grad_ref, coefs_ref, total_ref):
    coefs_ref[...] = merged_ref[0:8, :]
    grad_ref[...] = jnp.concatenate([merged_ref[8:9, :], merged_ref[9:10, :]], axis=1)
    total_ref[...] = merged_ref[10:11, :]


def per_device(
    features, fixed_coef, member_score, clicks, member_features, member_coef, block_slot
):
    n_dev = 128
    rows, width = features.shape
    vmem = pl.BlockSpec(memory_space=pltpu.VMEM)
    merged = pl.pallas_call(
        kernel,
        name="glmix",
        out_shape=pltpu.VMEM((16, 256), f32),
        in_specs=[pl.BlockSpec(memory_space=pltpu.HBM)] * 7,
        out_specs=vmem,
        scratch_shapes=[
            pltpu.VMEM((1, width), f32),
            pltpu.VMEM((rows // 128, 128), f32),
            pltpu.VMEM((rows // 128, 128), i32),
            pltpu.VMEM(member_features.shape, bf16),
            pltpu.VMEM(member_coef.shape, f32),
            pltpu.VMEM((1, 256), i32),
            pltpu.VMEM((rows, width), bf16),
            pltpu.VMEM((n_dev, 16, 128), bf16),
            pltpu.VMEM((n_dev, 16, 128), bf16),
            pltpu.VMEM((16, 1, 256), f32),
            pltpu.VMEM((16, 1, 256), f32),
            pltpu.VMEM((1, 256), f32),
            pltpu.VMEM((16, 1, 256), f32),
            pltpu.VMEM((n_dev, 1, 128), f32),
            pltpu.VMEM((n_dev, 1, 128), f32),
            pltpu.VMEM((8, 1, 128), f32),
            pltpu.VMEM((n_dev, 1, 128), f32),
            pltpu.VMEM((1, width), f32),
            pltpu.VMEM((8, 1, width), f32),
            pltpu.VMEM((n_dev, 256), bf16),
            pltpu.VMEM((1, 256), i32),
            pltpu.VMEM((1024, 256), bf16),
            pltpu.VMEM((128, 1024), bf16),
            pltpu.VMEM((512, 256), bf16),
            pltpu.VMEM((256, 128), f32),
            pltpu.SemaphoreType.DMA((6,)),
            pltpu.SemaphoreType.DMA((8,)),
            pltpu.SemaphoreType.DMA((6,)),
            pltpu.SemaphoreType.DMA((6,)),
        ],
        compiler_params=pltpu.CompilerParams(collective_id=0, has_side_effects=True),
    )(
        fixed_coef.reshape(1, width),
        member_score.reshape(rows // 128, 128),
        clicks.reshape(rows // 128, 128),
        member_features,
        member_coef,
        block_slot.reshape(1, -1),
        features,
    )
    grad, coefs, total = pl.pallas_call(
        split,
        name="split",
        out_shape=(
            jax.ShapeDtypeStruct((1, width), f32),
            jax.ShapeDtypeStruct(member_coef.shape, f32),
            jax.ShapeDtypeStruct((1, block_slot.shape[0]), f32),
        ),
        in_specs=[vmem],
        out_specs=(vmem,) * 3,
        compiler_params=pltpu.CompilerParams(vmem_limit_bytes=1 << 20),
    )(merged)
    return grad.reshape(-1), coefs, total.reshape(-1)


def solution(mesh):
    return jax.shard_map(
        per_device,
        mesh=mesh,
        in_specs=(
            P("dp", "feat"),
            P("feat"),
            P("dp"),
            P("dp"),
            P(("dp", "feat"), None),
            P(("dp", "feat"), None),
            P(("dp", "feat")),
        ),
        out_specs=(P("feat"), P(("dp", "feat"), None), P(("dp", "feat"))),
        check_vma=False,
    )
```
